32 devices in a mesh: band: 8 (over z, y), col: 4 (over x, core).
Axes of the slice: x: 2, y: 2, z: 4, core: 2. Of those that a mesh axis runs over, the one named last changes fastest.
Arguments:
- valence_wave: bfloat16 [16, 96, 9216], P('band', 'col'), may hold values from -6 to 6
- conduction_wave: bfloat16 [8, 96, 9216], P('band', 'col'), may hold values from -6 to 6
- valence_index: int32 [16], replicated, may hold values from 0 to 4095
- occupied_energy: float32 [4096], replicated, may hold values from -6 to -0.5
- conduction_energy: float32 [8], replicated, may hold values from 0.5 to 8
- frequency: float32 [4], replicated, may hold values from 0.5 to 16
- gvec_cell: int32 [8192], P('col'), may hold values from 0 to 221183, as said below
- block_cell: int32 [16], P('col'), may hold values from 0 to 221183, as said below
Outputs:
- chi: float32 [8192, 128], P(('col', 'band'))
The draws below stay inside these ranges and needn't reach their ends.
Inputs may be any that keep to these rules, and one draw needn't show every extreme that they name: `gvec_cell`: for rows j of owner k (k * 2048 <= j < (k + 1) * 2048) the entry is (kx 24 + ky - k * 24) * 96 + kz for the G vector's grid point (kx, ky, kz), whose ky lies in [k * 24, (k + 1) * 24); no point appears twice among the rows and block columns of one owner. `block_cell`: block column m has owner k = m // 4 and is encoded as for gvec_cell; its points differ from every row point of the same owner.
All inputs are finite; a program needn't handle non-finite values.
Results may differ from the reference program's by a relative error of at most 0.018.
Values may be sent and summed in bfloat16 or wider, within the bound.
A program may use at most 192 MiB of HBM per device.

```python
import math
import jax
import jax.numpy as jnp
from jax import lax

GX = 96
GY = 96
GZ = 96
G_DEV = 2048
NV = 16
NW = 4
NOCC = 4096
GB = 16
NG = 8192
NC = 8
PENCIL = 221184
GB_DEV = 4


def cell_lists(key):
    owners = NG // G_DEV
    keys = jax.random.split(jax.random.fold_in(key, 7), owners)
    return jax.vmap(lambda single: jax.random.permutation(single, PENCIL))(keys)


def draw_gvec_cell(key, part):
    lists = cell_lists(key)
    return lists[:, :G_DEV].reshape(-1).astype(jnp.int32)


def draw_block_cell(key, part):
    lists = cell_lists(key)
    return lists[:, G_DEV:G_DEV + GB_DEV].reshape(-1).astype(jnp.int32)


def set_ends(values, stream_key, low, high):
    longest = values.shape.index(max(values.shape))
    spots = []
    for shift in (0, 1):
        where = [jax.random.randint(jax.random.fold_in(stream_key, axis), (), 0, length) for axis, length in enumerate(values.shape)]
        where[longest] = (where[longest] + shift) % values.shape[longest]
        spots.append(tuple(where))
    return values.at[spots[0]].set(low).at[spots[1]].set(high)


def shard_levels(rng, extent, cuts, smallest, largest):
    factor_of, own = 1.0, jax.random.fold_in(rng, 6)
    for dim, parts in cuts:
        steps = jnp.exp(jax.random.uniform(jax.random.fold_in(own, dim), (parts,), jnp.float32, smallest / len(cuts), largest / len(cuts)))
        factor_of = factor_of * jnp.repeat(steps, extent[dim] // parts).reshape([-1 if axis == dim else 1 for axis in range(len(extent))])
    return factor_of


def bell_draw(stream_key, shape, scale, bound, cuts=(), kind=jnp.bfloat16):
    entries = jax.random.normal(stream_key, shape, jnp.float32) * scale
    if len(cuts) > 0:
        entries = shard_levels(stream_key, shape, cuts, -0.22, 0.18) * entries
    return jnp.clip(entries, min=-bound, max=bound).astype(kind)


def setup_inputs(seed: int = 0) -> dict:
    streams_of = jax.random.split(jax.random.key(seed), 9)
    return {
        "valence_wave": bell_draw(streams_of[0], (NV, GX, GY * GZ), 1.0, 6.0, ((0, 8), (1, 4))),
        "conduction_wave": bell_draw(streams_of[1], (NC, GX, GY * GZ), 1.0, 6.0, ((0, 8), (1, 4))),
        "valence_index": set_ends(jax.random.randint(streams_of[2], (NV,), 0, NOCC), jax.random.fold_in(streams_of[2], 1), 0, NOCC - 1).astype(jnp.int32),
        "occupied_energy": jnp.clip(jax.random.uniform(streams_of[3], (NOCC,), jnp.float32, -6.0, -0.5), -6.0, -0.5),
        "conduction_energy": jnp.clip(jax.random.uniform(streams_of[4], (NC,), jnp.float32, 0.5, 8.0), 0.5, 8.0),
        "frequency": jnp.clip(jnp.exp(jax.random.uniform(streams_of[5], (NW,), jnp.float32, math.log(0.5), math.log(16.0))), 0.5, 16.0),
        "gvec_cell": draw_gvec_cell(jax.random.fold_in(streams_of[8], 71), 0),
        "block_cell": draw_block_cell(jax.random.fold_in(streams_of[8], 71), 0),
    }


HIGHEST = lax.Precision.HIGHEST

def dft_tables(length, factor, out_type):
    indices = jnp.arange(length, dtype=jnp.int32)
    phases = indices[:, None] * indices[None, :] % length
    angles = phases.astype(jnp.float32) * (2.0 * math.pi / length)
    return ((jnp.cos(angles) * factor).astype(out_type), (-jnp.sin(angles) * factor).astype(out_type))

def weighted_columns(block, weights):
    columns = block.astype(jnp.float32)
    stacked = jnp.stack([columns, jnp.stack([-columns[1], columns[0]])])
    scaled = stacked[None] * weights[:, None, None, :, None]
    scaled = scaled.transpose(2, 3, 0, 1, 4).astype(jnp.bfloat16)
    return scaled.reshape(2, block.shape[1], -1)

def reference(valence_wave, conduction_wave, valence_index, occupied_energy, conduction_energy, frequency, gvec_cell, block_cell):
    col_count = NG // G_DEV
    slab_y = GY // col_count

    def grid_points(cells, per_owner):
        owner = jnp.arange(cells.shape[0], dtype=jnp.int32) // per_owner
        point_x = cells // (slab_y * GZ)
        point_y = owner * slab_y + cells // GZ % slab_y
        point_z = cells % GZ
        return (point_x, point_y, point_z)
    row_points = grid_points(gvec_cell, G_DEV)
    block_points = grid_points(block_cell, GB // col_count)
    x_cosine, x_sine = dft_tables(GX, 1.0 / math.sqrt(GX), jnp.bfloat16)
    cosine_full = x_cosine.astype(jnp.float32)
    sine_full = x_sine.astype(jnp.float32)
    valence_float = valence_wave.astype(jnp.float32).reshape(NV, GX, GY, GZ)

    def one_band(wave):
        products = valence_float * wave.astype(jnp.float32).reshape(GX, GY, GZ)[None]
        plane = jnp.fft.fft2(products, axes=(2, 3)) / math.sqrt(GY * GZ)
        plane_real = lax.optimization_barrier(jnp.real(plane).astype(jnp.bfloat16)).astype(jnp.float32)
        plane_imag = lax.optimization_barrier(jnp.imag(plane).astype(jnp.bfloat16)).astype(jnp.float32)
        real_part = jnp.einsum('kx,vxyz->vkyz', cosine_full, plane_real, precision=HIGHEST) - jnp.einsum('kx,vxyz->vkyz', sine_full, plane_imag, precision=HIGHEST)
        imag_part = jnp.einsum('kx,vxyz->vkyz', sine_full, plane_real, precision=HIGHEST) + jnp.einsum('kx,vxyz->vkyz', cosine_full, plane_imag, precision=HIGHEST)
        density_real = real_part.astype(jnp.bfloat16)
        density_imag = imag_part.astype(jnp.bfloat16)
        rows = jnp.stack([density_real[:, row_points[0], row_points[1], row_points[2]], density_imag[:, row_points[0], row_points[1], row_points[2]]])
        block = jnp.stack([density_real[:, block_points[0], block_points[1], block_points[2]], density_imag[:, block_points[0], block_points[1], block_points[2]]])
        return (rows, block)
    rows, blocks = lax.map(one_band, conduction_wave)
    row_density = jnp.transpose(rows, (1, 0, 2, 3)).reshape(2, NC * NV, NG)
    block_density = jnp.transpose(blocks, (1, 0, 2, 3)).reshape(2, NC * NV, GB)
    valence_energy = occupied_energy[valence_index]
    gap = (conduction_energy[:, None] - valence_energy[None, :]).reshape(-1)
    freq_column = frequency[:, None]
    weights = -4.0 * gap[None, :] / (gap[None, :] * gap[None, :] + freq_column * freq_column) * (1.0 / math.sqrt(NV * NC))
    right_side = weighted_columns(block_density, weights).reshape(2 * NC * NV, -1)
    left_side = jnp.transpose(row_density, (2, 0, 1)).reshape(NG, 2 * NC * NV)
    return jnp.dot(left_side, right_side, preferred_element_type=jnp.float32)
```

```python
import functools
import math

import jax
import jax.numpy as jnp
import numpy as np
from jax import lax
from jax.experimental import pallas as pl
from jax.experimental.pallas import tpu as pltpu
from jax.sharding import PartitionSpec as P

GY = 96
LANE = 128
SUB = 8
INNER = 2
STEPS = 4
MESH = pl.DeviceIdType.MESH
VMEM_LIMIT = 62 * 1024 * 1024


def up(n, k):
    return -(-n // k) * k


def rounded(a):
    return jnp.asarray(a, jnp.bfloat16)


def angles(rows, cols, length):
    return 2.0 * math.pi * ((np.outer(rows, cols) % length) / length)


class Plan:
    def __init__(self, v_own, c_own, slab_x, plane, cols, bands, rows_all, blocks_all):
        self.inner = INNER if bands % INNER == 0 else 1
        self.outer = bands // self.inner
        self.v_own, self.c_own = v_own, c_own
        self.nv, self.nc, self.slab_x = v_own * self.inner, c_own * self.outer, slab_x
        self.gy, self.gz, self.gx = GY, plane // GY, slab_x * cols
        self.cols, self.bands = cols, bands
        self.pairs = self.nv * self.nc
        self.lanes = self.pairs * slab_x
        self.lanes_pad = up(self.lanes, LANE)
        self.chunks = self.lanes_pad // LANE
        self.tile = up(2 * self.chunks, SUB)
        self.half = self.gz // 2 + 1
        self.zrows = up(2 * self.half, SUB)
        self.group_lanes = self.gz * LANE // math.gcd(self.gz, LANE)
        self.group = self.group_lanes // self.gz
        self.dests = cols * bands
        self.rows_dest = rows_all // self.dests
        self.pack = LANE // (2 * self.pairs)
        self.rows_packed = self.rows_dest // self.pack
        self.blocks = blocks_all
        self.steps = STEPS
        self.block_packed = up(blocks_all, self.pack) // self.pack
        self.block_rows = up(self.block_packed, 2 * SUB)
        self.code_split = up(self.gx + 1, LANE)

    def windows(self):
        out, y = [], 0
        while y < self.group:
            start = y * self.gz // LANE * LANE
            ys = []
            while y < self.group and (y + 1) * self.gz <= start + 2 * LANE:
                ys.append(y)
                y += 1
            width = up(ys[-1] * self.gz + self.gz - start, LANE)
            out.append((start, width, ys))
        return out

    def z_tables(self):
        ang = angles(np.arange(self.half), np.arange(self.gz), self.gz)
        one = np.zeros((self.zrows, self.gz), np.float32)
        one[: self.half] = np.cos(ang)
        one[self.half : 2 * self.half] = -np.sin(ang)
        tables = []
        for start, width, ys in self.windows():
            t = np.zeros((len(ys) * self.zrows, width), np.float32)
            for i, y in enumerate(ys):
                lo = y * self.gz - start
                t[i * self.zrows : (i + 1) * self.zrows, lo : lo + self.gz] = one
            tables.append(rounded(t))
        return tables

    def y_table(self):
        ang = angles(np.arange(self.gy), np.arange(self.gy), self.gy)
        scale = 1.0 / math.sqrt(self.gy * self.gz)
        cos, sin = np.cos(ang) * scale, -np.sin(ang) * scale
        return rounded(np.block([[cos, -sin], [sin, cos]]))

    def x_tables(self):
        wide = 2 * self.lanes_pad
        out = np.zeros((self.cols, self.code_split, wide + LANE), np.float32)
        out[:, : self.gx, wide:] = 1.0
        out[:, self.gx, wide + self.pairs :] = -2.0
        scale = 1.0 / math.sqrt(self.gx)
        for col in range(self.cols):
            xs = col * self.slab_x + np.arange(self.lanes) % self.slab_x
            ang = angles(np.arange(self.gx), xs, self.gx)
            out[col, : self.gx, : self.lanes] = np.cos(ang) * scale
            out[col, : self.gx, self.lanes_pad : self.lanes_pad + self.lanes] = -np.sin(ang) * scale
        return rounded(out)

    def fold_table(self):
        out = np.zeros((2 * self.lanes_pad, LANE), np.float32)
        n = np.arange(self.lanes)
        out[n, n // self.slab_x] = 1.0
        out[self.lanes_pad + n, self.pairs + n // self.slab_x] = 1.0
        return rounded(out)


def density_kernel(p, pidx, v_own, v_far, c_own, c_far, code_ref, *refs):
    n_win = len(p.windows())
    zt_refs = refs[:n_win]
    yt_ref, xt_ref, fold_ref, out_ref, z_ref, planes_ref, pick_ref, v_ref, c_ref, sem = refs[n_win:]
    f32, bf16 = jnp.float32, jnp.bfloat16
    sx = p.slab_x

    outer, inner = place(p)
    copies = []
    for own, far, dst, n, me in ((v_own, v_far, v_ref, p.inner, inner), (c_own, c_far, c_ref, p.outer, outer)):
        size = own.shape[0]
        for d in range(n):
            src = own if d == 0 else far.at[d - 1]
            slot = lax.rem(me + d, n) * size
            copies.append(pltpu.make_async_copy(src, dst.at[pl.ds(slot, size)], sem.at[len(copies)]))
    for copy in copies:
        copy.start()
    for copy in copies:
        copy.wait()

    def z_step(q, carry):
        lanes = pl.ds(pl.multiple_of(q * p.group_lanes, LANE), p.group_lanes)
        v = v_ref[:, :, lanes].astype(f32)
        c = c_ref[:, :, lanes].astype(f32)
        parts = [v[i] * c[j] for i in range(p.nv) for j in range(p.nc)]
        if p.lanes_pad > p.lanes:
            parts.append(jnp.zeros((p.lanes_pad - p.lanes, p.group_lanes), f32))
        prod = jnp.concatenate(parts, axis=0).astype(bf16)
        for t_ref, (start, width, ys) in zip(zt_refs, p.windows()):
            z = lax.dot_general(
                t_ref[...],
                prod[:, start : start + width],
                (((1,), (1,)), ((), ())),
                preferred_element_type=f32,
            )
            rows = len(ys) * p.zrows
            base = pl.multiple_of((q * p.group + ys[0]) * p.zrows, SUB)
            for j in range(p.chunks):
                z_ref[j, pl.ds(base, rows), :] = z[:, j * LANE : (j + 1) * LANE]
        return carry

    lax.fori_loop(0, p.gy // p.group, z_step, 0)

    def y_step(kz, carry):
        cols = []
        for j in range(p.chunks):
            parts = [
                z_ref[j, pl.ds(r * p.half + kz, p.gy, stride=p.zrows), :] for r in range(2)
            ]
            cols.append(jnp.concatenate(parts, axis=0).astype(bf16))
        rhs = jnp.concatenate(cols, axis=1)
        out = jnp.dot(yt_ref[...], rhs, preferred_element_type=f32)
        for s in range(2):
            for j in range(p.chunks):
                planes_ref[pl.ds(kz * (p.gy * p.tile) + s * p.chunks + j, p.gy, stride=p.tile), :] = out[
                    s * p.gy : (s + 1) * p.gy, j * LANE : (j + 1) * LANE
                ]
        return carry

    lax.fori_loop(0, p.half, y_step, 0)

    col = lax.axis_index("col")

    def density(d, rows):
        def pick(i, carry):
            for u in range(16):
                g = i * 16 + u
                src = pl.multiple_of(pidx[d * p.rows_dest + g], SUB)
                pick_ref[pl.ds(pl.multiple_of(g * p.tile, SUB), p.tile), :] = planes_ref[pl.ds(src, p.tile), :]
            return carry

        lax.fori_loop(0, rows // 16, pick, 0)
        code = code_ref[pl.ds(d, 1), :rows]
        mirror = code >= p.code_split
        kx = jnp.where(mirror, code - p.code_split, code)
        span = lax.broadcasted_iota(jnp.int32, (p.code_split, rows), 0)
        hot = jnp.where((span == kx) | ((span == p.gx) & mirror), 1.0, 0.0).astype(bf16)
        phase = lax.dot_general(
            hot, xt_ref[col], (((0,), (0,)), ((), ())), preferred_element_type=f32
        )
        real, imag = [], []
        for j in range(p.chunks):
            re = pick_ref[pl.ds(j, rows, stride=p.tile), :]
            im = pick_ref[pl.ds(p.chunks + j, rows, stride=p.tile), :]
            cos = phase[:, j * LANE : (j + 1) * LANE]
            sin = phase[:, p.lanes_pad + j * LANE : p.lanes_pad + (j + 1) * LANE]
            real.append((cos * re - sin * im).astype(bf16))
            imag.append((sin * re + cos * im).astype(bf16))
        turned = jnp.concatenate(real + imag, axis=1)
        folded = jnp.dot(turned, fold_ref[...], preferred_element_type=f32)
        return folded * phase[:, 2 * p.lanes_pad :]

    def packed(full, rows):
        step = rows // p.pack
        total = full[:step]
        for q in range(1, p.pack):
            total = total + pltpu.roll(full[q * step : (q + 1) * step], q * 2 * p.pairs, 1)
        return total

    def row_step(d, carry):
        out_ref[d] = packed(density(d, p.rows_dest), p.rows_dest).astype(bf16)
        return carry

    lax.fori_loop(0, p.dests + 1, row_step, 0)


def density_call(p, pidx, code, v_own, v_far, c_own, c_far):
    tables = p.z_tables() + [p.y_table(), p.x_tables(), p.fold_table()]
    vmem = pl.BlockSpec(memory_space=pltpu.VMEM)
    return pl.pallas_call(
        functools.partial(density_kernel, p),
        out_shape=jax.ShapeDtypeStruct((p.dests + 1, p.rows_packed, LANE), jnp.bfloat16),
        in_specs=[pl.BlockSpec(memory_space=pltpu.SMEM)]
        + [pl.BlockSpec(memory_space=pl.ANY)] * 4
        + [vmem] * (1 + len(tables)),
        out_specs=vmem,
        scratch_shapes=[
            pltpu.VMEM((p.chunks, p.gy * p.zrows, LANE), jnp.float32),
            pltpu.VMEM((p.half * p.gy * p.tile, LANE), jnp.float32),
            pltpu.VMEM((p.rows_dest * p.tile, LANE), jnp.float32),
            pltpu.VMEM((p.nv, p.slab_x, p.gy * p.gz), jnp.bfloat16),
            pltpu.VMEM((p.nc, p.slab_x, p.gy * p.gz), jnp.bfloat16),
            pltpu.SemaphoreType.DMA((p.inner + p.outer,)),
        ],
        compiler_params=pltpu.CompilerParams(vmem_limit_bytes=VMEM_LIMIT),
        name="density",
    )(pidx, v_own, v_far, c_own, c_far, code, *tables)


def lookups(p, cells, blocks):
    slab_y = p.gy // p.cols

    def points(values):
        owner = lax.broadcasted_iota(jnp.int32, values.shape, 0)
        kx = values // (slab_y * p.gz)
        ky = owner * slab_y + values // p.gz % slab_y
        kz = values % p.gz
        mirror = kz >= p.half
        kx = jnp.where(mirror & (kx > 0), p.gx - kx, kx)
        ky = jnp.where(mirror & (ky > 0), p.gy - ky, ky)
        kz = jnp.where(mirror, p.gz - kz, kz)
        return (kz * p.gy + ky) * p.tile, kx + jnp.where(mirror, p.code_split, 0)

    pencil, code = points(cells)
    m = np.arange(p.blocks)
    slot = m // p.block_packed * p.rows_packed + m % p.block_packed
    spread = np.zeros((p.rows_dest,), np.int32)
    spread[slot] = m
    hot = jnp.asarray(spread[None, :] == m[:, None])

    def last(a):
        return jnp.sum(jnp.where(hot, a.reshape(-1, 1), 0), axis=0)[None]

    block_pencil, block_code = points(blocks)
    pencil = jnp.concatenate([pencil.reshape(-1, p.rows_dest), last(block_pencil)], axis=0)
    code = jnp.concatenate([code.reshape(-1, p.rows_dest), last(block_code)], axis=0)
    return pencil.reshape(-1), code


def place(p):
    band = lax.axis_index("band")
    return band // p.inner, lax.rem(band, p.inner)


def meet(targets):
    barrier = pltpu.get_barrier_semaphore()
    for target in targets:
        pl.semaphore_signal(barrier, inc=1, device_id=target, device_id_type=MESH)
    pl.semaphore_wait(barrier, len(targets))


def gather_kernel(p, v_in, c_in, cell_in, block_in, v_out, c_out, cell_out, block_out, vs, vr, cs, cr, cell_sem):
    outer, inner = place(p)
    col = lax.axis_index("col")
    at = lambda o, i: (o * p.inner + i, col)
    lanes = v_in.shape[2] // p.steps

    def cut(ref, step):
        return ref.at[:, :, pl.ds(step * lanes, lanes)]

    inner_ids = [at(outer, lax.rem(inner + d, p.inner)) for d in range(1, p.inner)]
    up_id, down_id = (at(lax.rem(outer + s, p.outer), inner) for s in (1, p.outer - 1))
    col_ids = [(lax.axis_index("band"), lax.rem(col + d, p.cols)) for d in range(1, p.cols)]
    meet(inner_ids + [up_id, down_id] + col_ids)

    cell_copies = []
    for d, target in enumerate(col_ids):
        for k, (src, dst) in enumerate(((cell_in, cell_out), (block_in, block_out))):
            cell_copies.append(
                pltpu.make_async_remote_copy(
                    src, dst.at[col], cell_sem.at[0, d, k], cell_sem.at[1, d, k], device_id=target, device_id_type=MESH
                )
            )
    mine = [
        pltpu.make_async_copy(src, dst.at[col], cell_sem.at[0, p.cols - 1, k])
        for k, (src, dst) in enumerate(((cell_in, cell_out), (block_in, block_out)))
    ]
    v_copies = [
        [
            pltpu.make_async_remote_copy(
                cut(v_in, step),
                cut(v_out.at[p.inner - d - 1], step),
                vs.at[d - 1, step],
                vr.at[p.inner - d - 1, step],
                device_id=target,
                device_id_type=MESH,
            )
            for step in range(p.steps)
        ]
        for d, target in enumerate(inner_ids, 1)
    ]

    def hop(way, d, step):
        if way == 0:
            slot, target = p.outer - 1 - d - 1, up_id
            src = c_in if d == 0 else c_out.at[p.outer - d - 1]
        else:
            slot, target = d, down_id
            src = c_in if d == 0 else c_out.at[d - 1]
        return pltpu.make_async_remote_copy(
            cut(src, step),
            cut(c_out.at[slot], step),
            cs.at[way, d, step],
            cr.at[slot, step],
            device_id=target,
            device_id_type=MESH,
        )

    def sends(way, d):
        if way == 0:
            return (outer >= d) & (outer < p.outer - 1)
        return (outer + d < p.outer) & (outer > 0)

    def arrival(way, d, step):
        return hop(way, d - 1, step)

    for step in range(p.steps):
        for way in range(2):

            @pl.when(sends(way, 0))
            def _():
                hop(way, 0, step).start()

        for copies in v_copies:
            copies[step].start()
        if step == 0:
            for copy in cell_copies + mine:
                copy.start()
    for d in range(1, p.outer - 1):
        for step in range(p.steps):
            for way in range(2):

                @pl.when(sends(way, d))
                def _():
                    arrival(way, d, step).wait_recv()
                    hop(way, d, step).start()

    for way in range(2):
        for d in range(1, p.outer):
            last = (outer == p.outer - 1) if way == 0 else (outer == 0)

            @pl.when(last)
            def _():
                for step in range(p.steps):
                    arrival(way, d, step).wait_recv()

    for way in range(2):
        for d in range(p.outer - 1):

            @pl.when(sends(way, d))
            def _():
                for step in range(p.steps):
                    hop(way, d, step).wait_send()

    for copies in v_copies:
        for copy in copies:
            copy.wait()
    for copy in cell_copies + mine:
        copy.wait()


def gather_call(p, v, c, cells, blocks):
    hbm = pl.BlockSpec(memory_space=pl.ANY)
    dma = pltpu.SemaphoreType.DMA
    out = [
        jax.ShapeDtypeStruct((p.inner - 1,) + v.shape, v.dtype),
        jax.ShapeDtypeStruct((p.outer - 1,) + c.shape, c.dtype),
        jax.ShapeDtypeStruct((p.cols,) + cells.shape, cells.dtype),
        jax.ShapeDtypeStruct((p.cols,) + blocks.shape, blocks.dtype),
    ]
    return pl.pallas_call(
        functools.partial(gather_kernel, p),
        out_shape=out,
        in_specs=[hbm] * 4,
        out_specs=[hbm] * 4,
        scratch_shapes=[
            dma((p.inner - 1, p.steps)),
            dma((p.inner - 1, p.steps)),
            dma((2, p.outer - 1, p.steps)),
            dma((p.outer - 1, p.steps)),
            dma((2, p.cols, 2)),
        ],
        compiler_params=pltpu.CompilerParams(collective_id=0, has_side_effects=True),
        name="gather",
    )(v, c, cells, blocks)


def exchange_kernel(p, part_ref, row_out, block_out, send_sem, recv_sem):
    col, band = lax.axis_index("col"), lax.axis_index("band")
    me = col * p.bands + band

    def target(d):
        other = lax.rem(me + d, p.dests)
        return other, (lax.rem(other, p.bands), other // p.bands)

    barrier = pltpu.get_barrier_semaphore()

    def greet(d, carry):
        pl.semaphore_signal(barrier, inc=1, device_id=target(d)[1], device_id_type=MESH)
        return carry

    lax.fori_loop(1, p.dests, greet, 0)
    pl.semaphore_wait(barrier, p.dests - 1)

    def copies(d):
        other, where = target(d)
        tail = part_ref.at[p.dests, pl.ds(0, p.block_rows)]
        return [
            pltpu.make_async_remote_copy(
                src, dst, send_sem.at[d, k], recv_sem.at[d, k], device_id=where, device_id_type=MESH
            )
            for k, (src, dst) in enumerate(((part_ref.at[other], row_out.at[me]), (tail, block_out.at[me])))
        ]

    def start(d, carry):
        for copy in copies(d):
            copy.start()
        return carry

    lax.fori_loop(1, p.dests, start, 0)
    row_out[pl.ds(me, 1)] = part_ref[pl.ds(me, 1)]
    block_out[pl.ds(me, 1)] = part_ref[p.dests :, : p.block_rows]

    def finish(d, carry):
        for copy in copies(d):
            copy.wait()
        return carry

    lax.fori_loop(1, p.dests, finish, 0)


def exchange_call(p, part):
    vmem = pl.BlockSpec(memory_space=pltpu.VMEM)
    dma = pltpu.SemaphoreType.DMA
    return pl.pallas_call(
        functools.partial(exchange_kernel, p),
        out_shape=[
            jax.ShapeDtypeStruct((p.dests, p.rows_packed, LANE), part.dtype),
            jax.ShapeDtypeStruct((p.dests, p.block_rows, LANE), part.dtype),
        ],
        in_specs=[vmem],
        out_specs=[vmem, vmem],
        scratch_shapes=[dma((p.dests, 2)), dma((p.dests, 2))],
        compiler_params=pltpu.CompilerParams(collective_id=1, has_side_effects=True),
        name="exchange",
    )(part)


def polarizability(p, rows_in, blocks_in, weights):
    f32, bf16 = jnp.float32, jnp.bfloat16

    def total(parts):
        parts = parts.reshape((p.cols, p.bands) + parts.shape[1:]).astype(f32)
        return jnp.sum(parts, axis=0).astype(bf16)

    rows = total(rows_in)
    block = total(blocks_in)[:, : p.block_packed].astype(f32)
    block = block.reshape(p.bands, p.block_packed, p.pack, 2, p.pairs)
    block = block.transpose(0, 3, 4, 2, 1).reshape(p.bands, 2, p.pairs, p.pack * p.block_packed)[..., : p.blocks]
    real, imag = block[:, 0], block[:, 1]
    pair = jnp.stack([jnp.stack([real, -imag], axis=2), jnp.stack([imag, real], axis=2)], axis=1)
    right = pair[:, :, :, None] * weights.transpose(0, 2, 1)[:, None, :, :, None, None]
    right = right.astype(bf16).reshape(p.bands, 1, 2 * p.pairs, 1, -1)
    eye = jnp.asarray(np.eye(p.pack).reshape(1, p.pack, 1, p.pack, 1), bf16)
    right = (eye * right).reshape(p.bands * LANE, -1)
    left = rows.transpose(1, 0, 2).reshape(p.rows_packed, p.bands * LANE)
    chi = jnp.dot(left, right, preferred_element_type=f32)
    return chi.reshape(p.rows_packed, p.pack, -1).transpose(1, 0, 2).reshape(p.rows_dest, -1)


def pair_weights(p, valence_index, occupied_energy, conduction_energy, frequency):
    span = jnp.arange(occupied_energy.shape[0], dtype=jnp.int32)
    hit = valence_index[:, None] == span[None, :]
    valence_energy = jnp.sum(jnp.where(hit, occupied_energy[None, :], 0.0), axis=1)
    gap = conduction_energy[None, :] - valence_energy[:, None]
    freq = frequency[:, None, None]
    norm = 1.0 / math.sqrt(gap.size)
    weights = -4.0 * gap[None] / (gap[None] * gap[None] + freq * freq) * norm
    split = weights.reshape(-1, p.outer, p.nv, p.outer, p.inner, p.c_own)
    return split.transpose(1, 4, 0, 2, 3, 5).reshape(p.bands, -1, p.pairs)


def per_device(
    valence_wave,
    conduction_wave,
    valence_index,
    occupied_energy,
    conduction_energy,
    frequency,
    gvec_cell,
    block_cell,
):
    cols, bands = lax.axis_size("col"), lax.axis_size("band")
    p = Plan(
        valence_wave.shape[0],
        conduction_wave.shape[0],
        valence_wave.shape[1],
        valence_wave.shape[2],
        cols,
        bands,
        gvec_cell.shape[0] * cols,
        block_cell.shape[0] * cols,
    )
    weights = pair_weights(p, valence_index, occupied_energy, conduction_energy, frequency)
    v_far, c_far, cells, blocks = gather_call(
        p, valence_wave, conduction_wave, gvec_cell.reshape(-1, LANE), block_cell.reshape(1, -1)
    )
    pencil, code = lookups(p, cells.reshape(cols, -1), blocks.reshape(cols, -1))
    part = density_call(p, pencil, code, valence_wave, v_far, conduction_wave, c_far)
    rows, block = exchange_call(p, part)
    return polarizability(p, rows, block, weights)


def solution(mesh):
    return jax.shard_map(
        per_device,
        mesh=mesh,
        in_specs=(
            P("band", "col", None),
            P("band", "col", None),
            P(),
            P(),
            P(),
            P(),
            P("col"),
            P("col"),
        ),
        out_specs=P(("col", "band"), None),
        check_vma=False,
    )
```

```python
import functools
import math

import jax
import jax.numpy as jnp
import numpy as np
from jax import lax
from jax.experimental import pallas as pl
from jax.experimental.pallas import tpu as pltpu
from jax.sharding import PartitionSpec as P

GY = 96
LANE = 128
SUB = 8
INNER = 2
STEPS = 6
MESH = pl.DeviceIdType.MESH
VMEM_LIMIT = 66_000_000


def up(n, k):
    return -(-n // k) * k


def rounded(a):
    return jnp.asarray(a, jnp.bfloat16)


def angles(rows, cols, length):
    return 2.0 * math.pi * ((np.outer(rows, cols) % length) / length)


class Plan:
    def __init__(self, v_own, c_own, slab_x, plane, cols, bands, rows_all, blocks_all, freqs):
        self.inner = INNER if bands % INNER == 0 else 1
        self.outer = bands // self.inner
        self.v_own, self.c_own = v_own, c_own
        self.nv, self.nc, self.slab_x = v_own * self.inner, c_own * self.outer, slab_x
        self.gy, self.gz, self.gx = GY, plane // GY, slab_x * cols
        self.cols, self.bands, self.freqs = cols, bands, freqs
        self.pairs = self.nv * self.nc
        self.lanes = self.pairs * slab_x
        self.lanes_pad = up(self.lanes, LANE)
        self.chunks = self.lanes_pad // LANE
        self.tile = up(2 * self.chunks, SUB)
        self.pitch = self.tile + 1
        self.half = self.gz // 2 + 1
        self.zrows = up(2 * self.half, SUB)
        self.zpitch = self.zrows + 1
        self.group_lanes = self.gz * LANE // math.gcd(self.gz, LANE)
        self.group = self.group_lanes // self.gz
        self.dests = cols * bands
        self.rows_dest = rows_all // self.dests
        self.halves = self.rows_dest // LANE
        self.pack = LANE // (2 * self.pairs)
        self.rows_packed = self.rows_dest // self.pack
        self.cell_rows = rows_all // cols // LANE
        self.blocks = blocks_all
        self.block_rows = up(blocks_all, 2 * SUB)
        self.steps = STEPS
        self.code_rows = up(self.gx + 1, LANE)
        self.wide = 2 * self.lanes_pad + LANE

    def windows(self):
        out, y = [], 0
        while y < self.group:
            start = y * self.gz // LANE * LANE
            ys = []
            while y < self.group and (y + 1) * self.gz <= start + 2 * LANE:
                ys.append(y)
                y += 1
            width = up(ys[-1] * self.gz + self.gz - start, LANE)
            out.append((start, width, ys))
        return out

    def z_tables(self):
        ang = angles(np.arange(self.half), np.arange(self.gz), self.gz)
        one = np.zeros((self.zrows, self.gz), np.float32)
        one[: self.half] = np.cos(ang)
        one[self.half : 2 * self.half] = -np.sin(ang)
        tables = []
        for start, width, ys in self.windows():
            t = np.zeros((len(ys) * self.zrows, width), np.float32)
            for i, y in enumerate(ys):
                lo = y * self.gz - start
                t[i * self.zrows : (i + 1) * self.zrows, lo : lo + self.gz] = one
            tables.append(rounded(t))
        return tables

    def y_table(self):
        ang = angles(np.arange(self.gy), np.arange(self.gy), self.gy)
        scale = 1.0 / math.sqrt(self.gy * self.gz)
        cos, sin = np.cos(ang) * scale, -np.sin(ang) * scale
        return rounded(np.block([[cos, -sin], [sin, cos]]))

    def x_tables(self):
        wide = 2 * self.lanes_pad
        out = np.zeros((self.cols, self.code_rows, wide + LANE), np.float32)
        out[:, : self.gx, wide:] = 1.0
        out[:, self.gx, wide + self.pairs :] = -2.0
        scale = 1.0 / math.sqrt(self.gx)
        for col in range(self.cols):
            xs = col * self.slab_x + np.arange(self.lanes) % self.slab_x
            ang = angles(np.arange(self.gx), xs, self.gx)
            out[col, : self.gx, : self.lanes] = np.cos(ang) * scale
            out[col, : self.gx, self.lanes_pad : self.lanes_pad + self.lanes] = -np.sin(ang) * scale
        return rounded(out)

    def fold_table(self):
        out = np.zeros((2 * self.lanes_pad, LANE), np.float32)
        n = np.arange(self.lanes)
        out[n, n // self.slab_x] = 1.0
        out[self.lanes_pad + n, self.pairs + n // self.slab_x] = 1.0
        return rounded(out)


def place(p):
    band = lax.axis_index("band")
    return band // p.inner, lax.rem(band, p.inner)


def remote(src, dst, send, recv, target):
    return pltpu.make_async_remote_copy(src, dst, send, recv, device_id=target, device_id_type=MESH)


def kernel(p, v_in, c_in, cell_in, xt_in, weight_ref, *refs):
    n_win = len(p.windows())
    zt_refs = refs[:n_win]
    (yt_ref, fold_ref, chi_ref, z_ref, planes_ref, pick_a, pick_b, v_ref, c_ref, cells, pidx_v, pidx, code_ref,
     phase_ref, xt_ref, part_ref, row_ref, block_ref, own_sem, vs, vr, cs, cr, cell_sem, row_sem, block_sem) = refs[n_win:]
    f32, bf16, i32 = jnp.float32, jnp.bfloat16, jnp.int32
    outer, inner = place(p)
    col, band = lax.axis_index("col"), lax.axis_index("band")
    me = col * p.bands + band

    def device(d):
        return (lax.rem(d, p.bands), d // p.bands)

    barrier = pltpu.get_barrier_semaphore()

    def greet(k, carry):
        target = device(lax.rem(me + k, p.dests))
        pl.semaphore_signal(barrier, inc=1, device_id=target, device_id_type=MESH)
        return carry

    lax.fori_loop(1, p.dests, greet, 0)
    local = [
        pltpu.make_async_copy(v_in, v_ref.at[pl.ds(inner * p.v_own, p.v_own)], own_sem.at[0]),
        pltpu.make_async_copy(c_in, c_ref.at[pl.ds(outer * p.c_own, p.c_own)], own_sem.at[1]),
        pltpu.make_async_copy(cell_in, cells.at[col], own_sem.at[2]),
        pltpu.make_async_copy(xt_in.at[col], xt_ref, own_sem.at[3]),
    ]
    for copy in local:
        copy.start()
    pl.semaphore_wait(barrier, p.dests - 1)

    step_lanes = p.gy * p.gz // p.steps

    def cut(ref, step):
        return ref.at[:, :, pl.ds(step * step_lanes, step_lanes)]

    def v_copy(d, step):
        slot = v_ref.at[pl.ds(inner * p.v_own, p.v_own)]
        target = (outer * p.inner + lax.rem(inner + d, p.inner), col)
        return remote(cut(v_in, step), cut(slot, step), vs.at[d - 1, step], vr.at[d - 1, step], target)

    def hop(way, d, step):
        origin = lax.rem(outer + (p.outer - d if way == 0 else d), p.outer)
        slot = c_ref.at[pl.ds(origin * p.c_own, p.c_own)]
        target = (lax.rem(outer + (1 if way == 0 else p.outer - 1), p.outer) * p.inner + inner, col)
        src = c_in if d == 0 else slot
        return remote(cut(src, step), cut(slot, step), cs.at[way, d, step], cr.at[way, d, step], target)

    def arrives(way, d, step):
        origin = lax.rem(outer + (p.outer - d if way == 0 else d), p.outer)
        slot = c_ref.at[pl.ds(origin * p.c_own, p.c_own)]
        return remote(cut(slot, step), cut(slot, step), cs.at[way, d - 1, step], cr.at[way, d - 1, step], (band, col))

    reach = (p.outer - 1) // 2

    def ways(d, step):
        if d <= reach:
            return (0, 1)
        return (step % 2,) if 2 * d == p.outer else ()

    far = p.outer // 2
    cell_copies = []
    for d in range(1, p.cols):
        target = (band, lax.rem(col + d, p.cols))
        cell_copies.append(remote(cell_in, cells.at[col], cell_sem.at[0, d - 1], cell_sem.at[1, d - 1], target))
    for copy in cell_copies:
        copy.start()
    for step in range(p.steps):
        for way in ways(1, step):
            hop(way, 0, step).start()
        for d in range(1, p.inner):
            v_copy(d, step).start()

    for copy in local[2:]:
        copy.wait()
    for copy in cell_copies:
        copy.wait()
    slab_y = p.gy // p.cols

    def points(values, owner):
        def split(a, n):
            high = lax.div(a, jnp.full(a.shape, n, i32))
            return high, a - high * n

        kx, rest = split(values, slab_y * p.gz)
        ky, kz = split(rest, p.gz)
        ky = ky + owner * slab_y
        mirror = kz >= p.half
        kx = jnp.where(mirror & (kx > 0), p.gx - kx, kx)
        ky = jnp.where(mirror & (ky > 0), p.gy - ky, ky)
        kz = jnp.where(mirror, p.gz - kz, kz)
        return (kz * p.gy + ky) * p.pitch, kx + jnp.where(mirror, p.code_rows, 0)

    last = jnp.zeros((1, LANE), i32)
    lane_owner = jnp.zeros((1, LANE), i32)
    lane = lax.broadcasted_iota(i32, (1, LANE), 1)
    per_owner = p.blocks // p.cols
    for k in range(p.cols):
        rows = pl.ds(k * p.cell_rows, p.cell_rows)
        pencil, code = points(cells[k, : p.cell_rows, :], k)
        pidx_v[rows, :] = pencil
        code_ref[rows, :] = code
        row = cells[k, p.cell_rows : p.cell_rows + 1, :]
        last = last + (pltpu.roll(row, k * per_owner, 1) if k else row)
        lane_owner = lane_owner + jnp.where(lane >= k * per_owner, 1, 0)
    pencil, code = points(last, jnp.minimum(lane_owner - 1, p.cols - 1))
    for k in range(p.halves):
        at = p.dests * p.halves + k
        pidx_v[pl.ds(at, 1), :] = pencil
        code_ref[pl.ds(at, 1), :] = code
    to_scalar = pltpu.make_async_copy(pidx_v, pidx, own_sem.at[4])

    def phases(i, carry):
        code = code_ref[pl.ds(i, 1), :]
        mirror = code >= p.code_rows
        kx = jnp.where(mirror, code - p.code_rows, code)
        span = lax.broadcasted_iota(i32, (p.code_rows, LANE), 0)
        hot = jnp.where((span == kx) | ((span == p.gx) & mirror), 1.0, 0.0).astype(bf16)
        phase = lax.dot_general(hot, xt_ref[...], (((0,), (0,)), ((), ())), preferred_element_type=f32)
        phase_ref[pl.ds(pl.multiple_of(i * LANE, LANE), LANE), :] = phase.astype(bf16)
        return carry

    groups = p.gy // p.group // p.steps

    def z_step(q, carry):
        lanes = pl.ds(pl.multiple_of(q * p.group_lanes, LANE), p.group_lanes)
        v = v_ref[:, :, lanes].astype(f32)
        c = c_ref[:, :, lanes].astype(f32)
        parts = [v[i] * c[j] for i in range(p.nv) for j in range(p.nc)]
        if p.lanes_pad > p.lanes:
            parts.append(jnp.zeros((p.lanes_pad - p.lanes, p.group_lanes), f32))
        prod = jnp.concatenate(parts, axis=0).astype(bf16)
        for t_ref, (start, width, ys) in zip(zt_refs, p.windows()):
            z = lax.dot_general(
                t_ref[...],
                prod[:, start : start + width],
                (((1,), (1,)), ((), ())),
                preferred_element_type=f32,
            )
            for j in range(p.chunks):
                for i, y in enumerate(ys):
                    base = (q * p.group + y) * p.zpitch
                    z_ref[j, pl.ds(base, p.zrows), :] = z[i * p.zrows : (i + 1) * p.zrows, j * LANE : (j + 1) * LANE]
        return carry

    halves_all = (p.dests + 1) * p.halves
    for step in range(p.steps + 1):
        if step < p.steps:
            lax.fori_loop(halves_all * step // p.steps, halves_all * (step + 1) // p.steps, phases, 0)
            if step == 0:
                to_scalar.start()
            for d in range(1, far):
                for way in ways(d, step):
                    arrives(way, d, step).wait_recv()
                for way in ways(d + 1, step):
                    hop(way, d, step).start()
        if step > 0:
            if step == 1:
                for copy in local[:2]:
                    copy.wait()
            for way in ways(far, step - 1):
                arrives(way, far, step - 1).wait_recv()
            for d in range(1, p.inner):
                v_copy(d, step - 1).wait_recv()
            lax.fori_loop(groups * (step - 1), groups * step, z_step, 0)
    to_scalar.wait()

    def y_step(kz, carry):
        cols = []
        for j in range(p.chunks):
            parts = [z_ref[j, pl.ds(r * p.half + kz, p.gy, stride=p.zpitch), :] for r in range(2)]
            cols.append(jnp.concatenate(parts, axis=0).astype(bf16))
        rhs = jnp.concatenate(cols, axis=1)
        out = jnp.dot(yt_ref[...], rhs, preferred_element_type=f32)
        for s in range(2):
            for j in range(p.chunks):
                to = pl.ds(kz * (p.gy * p.pitch) + s * p.chunks + j, p.gy, stride=p.pitch)
                planes_ref[to, :] = out[s * p.gy : (s + 1) * p.gy, j * LANE : (j + 1) * LANE]
        return carry

    lax.fori_loop(0, p.half, y_step, 0)

    def number(i):
        if isinstance(i, int):
            return p.dests if i == 0 else lax.rem(me + i, p.dests)
        return jnp.where(i == 0, p.dests, lax.rem(me + i, p.dests))

    def pick(i, buf):
        at = number(i) * p.halves
        for g in range(p.rows_dest):
            src = pidx[at + g // LANE, g % LANE]
            buf[pl.ds(g * p.pitch, p.tile), :] = planes_ref[pl.ds(src, p.tile), :]

    def turn(i, buf):
        d = number(i)
        rows = pl.ds(pl.multiple_of(d * p.rows_dest, LANE), p.rows_dest)
        real, imag = [], []
        for j in range(p.chunks):
            re = buf[pl.ds(j, p.rows_dest, stride=p.pitch), :]
            im = buf[pl.ds(p.chunks + j, p.rows_dest, stride=p.pitch), :]
            cos = phase_ref[rows, j * LANE : (j + 1) * LANE].astype(f32)
            sin = phase_ref[rows, p.lanes_pad + j * LANE : p.lanes_pad + (j + 1) * LANE].astype(f32)
            real.append((cos * re - sin * im).astype(bf16))
            imag.append((sin * re + cos * im).astype(bf16))
        turned = jnp.concatenate(real + imag, axis=1)
        folded = jnp.dot(turned, fold_ref[...], preferred_element_type=f32)
        folded = folded * phase_ref[rows, 2 * p.lanes_pad :].astype(f32)
        total = folded[: p.rows_packed]
        for q in range(1, p.pack):
            total = total + pltpu.roll(folded[q * p.rows_packed : (q + 1) * p.rows_packed], q * 2 * p.pairs, 1)
        part_ref[d] = total.astype(bf16)

    def row_copy(k):
        to = lax.rem(me + k, p.dests)
        return remote(part_ref.at[to], row_ref.at[me], row_sem.at[0, k], row_sem.at[1, k], device(to))

    def block_copy(k):
        to = lax.rem(me + k, p.dests)
        src = part_ref.at[p.dests, pl.ds(0, p.block_rows)]
        return remote(src, block_ref.at[me], block_sem.at[0, k], block_sem.at[1, k], device(to))

    def send(k):
        @pl.when(k > 0)
        def _():
            row_copy(k).start()
            block_copy(k).start()

    pick(0, pick_a)

    def walk(j, carry):
        pick(2 * j + 1, pick_b)
        turn(2 * j, pick_a)
        send(2 * j - 1)
        pick(2 * j + 2, pick_a)
        turn(2 * j + 1, pick_b)
        send(2 * j)
        return carry

    lax.fori_loop(0, p.dests // 2, walk, 0)
    send(p.dests - 1)
    turn(p.dests, pick_a)
    row_ref[pl.ds(me, 1)] = part_ref[pl.ds(me, 1)]
    block_ref[pl.ds(me, 1)] = part_ref[p.dests :, : p.block_rows]

    for step in range(p.steps):
        for d in range(far):
            for way in ways(d + 1, step):
                hop(way, d, step).wait_send()
        for d in range(1, p.inner):
            v_copy(d, step).wait_send()

    def finish(k, carry):
        row_copy(k).wait()
        block_copy(k).wait()
        return carry

    lax.fori_loop(1, p.dests, finish, 0)

    def added(ref, b):
        total = ref[b].astype(f32)
        for k in range(1, p.cols):
            total = total + ref[k * p.bands + b].astype(f32)
        return total.astype(bf16)

    pair_lane = lax.broadcasted_iota(i32, (1, LANE), 1)
    group_lanes = 2 * p.pairs
    acc = [jnp.zeros((p.rows_packed, 2 * p.freqs * p.blocks), f32) for _ in range(p.pack)]
    for b in range(p.bands):
        rows = added(row_ref, b)
        block = added(block_ref, b).astype(f32)[: p.blocks]
        first = jnp.where(pair_lane < group_lanes, block, 0.0)
        turned = jnp.where(
            pair_lane < p.pairs,
            -pltpu.roll(first, LANE - p.pairs, 1),
            jnp.where(pair_lane < group_lanes, pltpu.roll(first, p.pairs, 1), 0.0),
        )
        parts = []
        for w in range(p.freqs):
            weight = weight_ref[b, w : w + 1, :]
            parts += [weight * first, weight * turned]
        right = jnp.concatenate(parts, axis=0)
        for q in range(p.pack):
            shifted = (pltpu.roll(right, q * group_lanes, 1) if q else right).astype(bf16)
            acc[q] = acc[q] + lax.dot_general(
                rows, shifted, (((1,), (1,)), ((), ())), preferred_element_type=f32
            )
    for q in range(p.pack):
        chi_ref[q * p.rows_packed : (q + 1) * p.rows_packed, :] = acc[q]


def run(p, v, c, cells, weights):
    tables = p.z_tables() + [p.y_table(), p.fold_table()]
    vmem, hbm = pl.BlockSpec(memory_space=pltpu.VMEM), pl.BlockSpec(memory_space=pl.ANY)
    dma = pltpu.SemaphoreType.DMA
    f32, bf16, i32 = jnp.float32, jnp.bfloat16, jnp.int32
    halves_all = (p.dests + 1) * p.halves
    return pl.pallas_call(
        functools.partial(kernel, p),
        out_shape=jax.ShapeDtypeStruct((p.rows_dest, 2 * p.freqs * p.blocks), f32),
        in_specs=[hbm] * 4 + [vmem] * (1 + len(tables)),
        out_specs=vmem,
        scratch_shapes=[
            pltpu.VMEM((p.chunks, (p.gy + 1) * p.zpitch, LANE), f32),
            pltpu.VMEM(((p.half * p.gy + 1) * p.pitch, LANE), f32),
            pltpu.VMEM(((p.rows_dest + 1) * p.pitch, LANE), f32),
            pltpu.VMEM(((p.rows_dest + 1) * p.pitch, LANE), f32),
            pltpu.VMEM((p.nv, p.slab_x, p.gy * p.gz), bf16),
            pltpu.VMEM((p.nc, p.slab_x, p.gy * p.gz), bf16),
            pltpu.VMEM((p.cols,) + cells.shape, i32),
            pltpu.VMEM((halves_all, LANE), i32),
            pltpu.SMEM((halves_all, LANE), i32),
            pltpu.VMEM((halves_all, LANE), i32),
            pltpu.VMEM((halves_all * LANE, p.wide), bf16),
            pltpu.VMEM((p.code_rows, p.wide), bf16),
            pltpu.VMEM((p.dests + 1, p.rows_packed, LANE), bf16),
            pltpu.VMEM((p.dests, p.rows_packed, LANE), bf16),
            pltpu.VMEM((p.dests, p.block_rows, LANE), bf16),
            dma((5,)),
            dma((p.inner - 1, p.steps)),
            dma((p.inner - 1, p.steps)),
            dma((2, p.outer // 2, p.steps)),
            dma((2, p.outer // 2, p.steps)),
            dma((2, p.cols - 1)),
            dma((2, p.dests)),
            dma((2, p.dests)),
        ],
        compiler_params=pltpu.CompilerParams(
            collective_id=0, has_side_effects=True, vmem_limit_bytes=VMEM_LIMIT
        ),
        name="chi",
    )(v, c, cells, p.x_tables(), weights, *tables)


def pair_weights(p, valence_index, occupied_energy, conduction_energy, frequency):
    span = jnp.arange(occupied_energy.shape[0], dtype=jnp.int32)
    hit = valence_index[:, None] == span[None, :]
    valence_energy = jnp.sum(jnp.where(hit, occupied_energy[None, :], 0.0), axis=1)
    gap = conduction_energy[None, :] - valence_energy[:, None]
    freq = frequency[:, None, None]
    norm = 1.0 / math.sqrt(gap.size)
    weights = -4.0 * gap[None] / (gap[None] * gap[None] + freq * freq) * norm
    split = weights.reshape(-1, p.outer, p.nv, p.outer, p.inner, p.c_own)
    split = split.transpose(1, 4, 0, 2, 3, 5).reshape(p.bands, -1, p.pairs)
    return jnp.tile(split, (1, 1, LANE // p.pairs))


def per_device(
    valence_wave,
    conduction_wave,
    valence_index,
    occupied_energy,
    conduction_energy,
    frequency,
    gvec_cell,
    block_cell,
):
    cols, bands = lax.axis_size("col"), lax.axis_size("band")
    p = Plan(
        valence_wave.shape[0],
        conduction_wave.shape[0],
        valence_wave.shape[1],
        valence_wave.shape[2],
        cols,
        bands,
        gvec_cell.shape[0] * cols,
        block_cell.shape[0] * cols,
        frequency.shape[0],
    )
    weights = pair_weights(p, valence_index, occupied_energy, conduction_energy, frequency)
    tail = jnp.pad(block_cell, (0, SUB * LANE - block_cell.shape[0]))
    cells = jnp.concatenate([gvec_cell, tail]).reshape(-1, LANE)
    return run(p, valence_wave, conduction_wave, cells, weights)


def solution(mesh):
    return jax.shard_map(
        per_device,
        mesh=mesh,
        in_specs=(
            P("band", "col", None),
            P("band", "col", None),
            P(),
            P(),
            P(),
            P(),
            P("col"),
            P("col"),
        ),
        out_specs=P(("col", "band"), None),
        check_vma=False,
    )
```

```python
import functools
import math

import jax
import jax.numpy as jnp
import numpy as np
from jax import lax
from jax.experimental import pallas as pl
from jax.experimental.pallas import tpu as pltpu
from jax.sharding import PartitionSpec as P

GY = 96
LANE = 128
SUB = 8
INNER = 2
STEPS = 6
UNROLL_PHASE = 4
UNROLL_Y = 7
UNROLL_Z = 2
MESH = pl.DeviceIdType.MESH
VMEM_LIMIT = 66_000_000


def up(n, k):
    return -(-n // k) * k


def rounded(a):
    return jnp.asarray(a, jnp.bfloat16)


def angles(rows, cols, length):
    return 2.0 * math.pi * ((np.outer(rows, cols) % length) / length)


class Plan:
    def __init__(self, v_own, c_own, slab_x, plane, cols, bands, rows_all, blocks_all, freqs):
        self.inner = INNER if bands % INNER == 0 else 1
        self.outer = bands // self.inner
        self.v_own, self.c_own = v_own, c_own
        self.nv, self.nc, self.slab_x = v_own * self.inner, c_own * self.outer, slab_x
        self.gy, self.gz, self.gx = GY, plane // GY, slab_x * cols
        self.cols, self.bands, self.freqs = cols, bands, freqs
        self.pairs = self.nv * self.nc
        self.merge = max(1, min(self.outer, LANE // (c_own * self.nv * slab_x)))
        if self.outer % self.merge:
            self.merge = 1
        self.chunks = self.outer // self.merge
        self.chunk_pairs = self.pairs // self.chunks
        self.lanes = self.chunk_pairs * slab_x
        self.tile = up(2 * self.chunks, SUB)
        self.pitch = self.tile + 1
        self.half = self.gz // 2 + 1
        self.zrows = up(2 * self.half, SUB)
        self.zpitch = self.zrows + 1
        self.group_lanes = self.gz * LANE // math.gcd(self.gz, LANE)
        self.group = self.group_lanes // self.gz
        self.dests = cols * bands
        self.rows_dest = rows_all // self.dests
        self.halves = self.rows_dest // LANE
        self.pack = LANE // (2 * self.pairs)
        self.rows_packed = self.rows_dest // self.pack
        self.cell_rows = rows_all // cols // LANE
        self.blocks = blocks_all
        self.block_rows = up(blocks_all, 2 * SUB)
        self.steps = STEPS
        self.code_rows = up(self.gx + 1, LANE)
        self.wide = 3 * LANE
        self.valences, self.conductions = v_own * bands, c_own * bands

    def stages(self):
        if self.merge > 1:
            return [list(range(self.chunks))]
        return [list(range(k, min(k + 2, self.chunks))) for k in range(0, self.chunks, 2)]

    def arrivals(self, at):
        return sorted(range(self.outer), key=lambda o: (abs(o - at), o))

    def windows(self):
        out, y = [], 0
        while y < self.group:
            start = y * self.gz // LANE * LANE
            ys = []
            while y < self.group and (y + 1) * self.gz <= start + 2 * LANE:
                ys.append(y)
                y += 1
            width = up(ys[-1] * self.gz + self.gz - start, LANE)
            out.append((start, width, ys))
        return out

    def z_tables(self):
        ang = angles(np.arange(self.half), np.arange(self.gz), self.gz)
        one = np.zeros((self.zrows, self.gz), np.float32)
        one[: self.half] = np.cos(ang)
        one[self.half : 2 * self.half] = -np.sin(ang)
        tables = []
        for start, width, ys in self.windows():
            t = np.zeros((len(ys) * self.zrows, width), np.float32)
            for i, y in enumerate(ys):
                lo = y * self.gz - start
                t[i * self.zrows : (i + 1) * self.zrows, lo : lo + self.gz] = one
            tables.append(rounded(t))
        return tables

    def y_table(self):
        ang = angles(np.arange(self.gy), np.arange(self.gy), self.gy)
        scale = 1.0 / math.sqrt(self.gy * self.gz)
        cos, sin = np.cos(ang) * scale, -np.sin(ang) * scale
        return rounded(np.block([[cos, -sin], [sin, cos]]))

    def x_tables(self):
        out = np.zeros((self.cols, self.code_rows, self.wide), np.float32)
        out[:, : self.gx, 2 * LANE :] = 1.0
        out[:, self.gx, 2 * LANE + self.pairs :] = -2.0
        scale = 1.0 / math.sqrt(self.gx)
        for col in range(self.cols):
            xs = col * self.slab_x + np.arange(self.lanes) % self.slab_x
            ang = angles(np.arange(self.gx), xs, self.gx)
            out[col, : self.gx, : self.lanes] = np.cos(ang) * scale
            out[col, : self.gx, LANE : LANE + self.lanes] = -np.sin(ang) * scale
        return rounded(out)

    def fold_table(self):
        out = np.zeros((2 * LANE, LANE), np.float32)
        n = np.arange(self.lanes)
        out[n, n // self.slab_x] = 1.0
        out[LANE + n, self.pairs + n // self.slab_x] = 1.0
        return rounded(out)


def place(p):
    band = lax.axis_index("band")
    return band // p.inner, lax.rem(band, p.inner)


def remote(src, dst, send, recv, target):
    return pltpu.make_async_remote_copy(src, dst, send, recv, device_id=target, device_id_type=MESH)


def kernel(p, index_in, energy_in, conduction_in, freq_in, v_in, c_in, cell_in, block_in, xt_in, *refs):
    n_win = len(p.windows())
    zt_refs = refs[:n_win]
    (yt_ref, fold_ref, chi_ref, z_ref, planes_ref, pick_a, pick_b, v_ref, c_ref, cells, blocks_v, blocks, pidx_v, pidx, code_ref,
     phase_ref, xt_ref, part_ref, row1, sum_ref, row_ref, block1, block_ref, own_sem, vs, vr, cs, cr, cell_sem, sem1, sem2, met) = refs[n_win:]
    f32, bf16, i32 = jnp.float32, jnp.bfloat16, jnp.int32
    outer, inner = place(p)
    col, band = lax.axis_index("col"), lax.axis_index("band")
    line = [(outer > 0, outer - 1), (outer < p.outer - 1, outer + 1)]
    near = [(band, lax.rem(col + d, p.cols)) for d in range(1, p.cols)]
    near += [(outer * p.inner + lax.rem(inner + d, p.inner), col) for d in range(1, p.inner)]
    greeted = len(near) + sum(jnp.where(there, 1, 0) for there, _ in line)

    barrier = pltpu.get_barrier_semaphore()
    for target in near:
        pl.semaphore_signal(barrier, inc=1, device_id=target, device_id_type=MESH)
    for there, o in line:

        @pl.when(there)
        def _():
            pl.semaphore_signal(barrier, inc=1, device_id=(o * p.inner + inner, col), device_id_type=MESH)

    local = [
        pltpu.make_async_copy(v_in, v_ref.at[pl.ds(inner * p.v_own, p.v_own)], own_sem.at[0]),
        pltpu.make_async_copy(c_in, c_ref.at[pl.ds(outer * p.c_own, p.c_own)], own_sem.at[1]),
        pltpu.make_async_copy(cell_in, cells.at[col], own_sem.at[2]),
        pltpu.make_async_copy(xt_in.at[col], xt_ref, own_sem.at[3]),
        pltpu.make_async_copy(block_in, blocks_v.at[col], own_sem.at[4]),
    ]
    for copy in local:
        copy.start()
    pl.semaphore_wait(barrier, greeted)

    step_lanes = p.gy * p.gz // p.steps

    def cut(ref, step):
        return ref.at[:, :, pl.ds(step * step_lanes, step_lanes)]

    def v_copy(d, step):
        slot = v_ref.at[pl.ds(inner * p.v_own, p.v_own)]
        target = (outer * p.inner + lax.rem(inner + d, p.inner), col)
        return remote(cut(v_in, step), cut(slot, step), vs.at[d - 1, step], vr.at[d - 1, step], target)

    def hop(way, d, step):
        slot = c_ref.at[pl.ds((outer - d if way == 0 else outer + d) * p.c_own, p.c_own)]
        target = ((outer + (1 if way == 0 else -1)) * p.inner + inner, col)
        src = c_in if d == 0 else slot
        return remote(cut(src, step), cut(slot, step), cs.at[way, d, step], cr.at[way, d, step], target)

    def arrives(way, d, step):
        slot = c_ref.at[pl.ds((outer - d if way == 0 else outer + d) * p.c_own, p.c_own)]
        return remote(cut(slot, step), cut(slot, step), cs.at[way, d - 1, step], cr.at[way, d - 1, step], (band, col))

    def passes(way, d):
        if way == 0:
            return (outer >= d) & (outer < p.outer - 1)
        return (outer + d < p.outer) & (outer > 0)

    def pass_on(d, step):
        for way in range(2):

            @pl.when(passes(way, d))
            def _():
                if d > 0:
                    arrives(way, d, step).wait_recv()
                hop(way, d, step).start()

    def wait_ends(d, step):
        @pl.when(outer == p.outer - 1)
        def _():
            arrives(0, d, step).wait_recv()

        @pl.when(outer == 0)
        def _():
            arrives(1, d, step).wait_recv()

    cell_copies = []
    for d in range(1, p.cols):
        target = (band, lax.rem(col + d, p.cols))
        cell_copies.append(remote(cell_in, cells.at[col], cell_sem.at[0, 0, d - 1], cell_sem.at[1, 0, d - 1], target))
        cell_copies.append(remote(block_in, blocks_v.at[col], cell_sem.at[0, 1, d - 1], cell_sem.at[1, 1, d - 1], target))
    for copy in cell_copies:
        copy.start()
    for step in range(p.steps):
        pass_on(0, step)
        for d in range(1, p.inner):
            v_copy(d, step).start()

    for copy in local[2:]:
        copy.wait()
    for copy in cell_copies:
        copy.wait()
    to_scalar = pltpu.make_async_copy(blocks_v, blocks, own_sem.at[5])
    to_scalar.start()
    slab_y = p.gy // p.cols

    def points(values, owner):
        def split(a, n):
            high = lax.div(a, jnp.full(a.shape, n, i32))
            return high, a - high * n

        kx, rest = split(values, slab_y * p.gz)
        ky, kz = split(rest, p.gz)
        ky = ky + owner * slab_y
        mirror = kz >= p.half
        kx = jnp.where(mirror & (kx > 0), p.gx - kx, kx)
        ky = jnp.where(mirror & (ky > 0), p.gy - ky, ky)
        kz = jnp.where(mirror, p.gz - kz, kz)
        return (kz * p.gy + ky) * p.pitch, kx + jnp.where(mirror, p.code_rows, 0)

    for k in range(p.cols):
        rows = pl.ds(k * p.cell_rows, p.cell_rows)
        pidx_v[rows, :], code_ref[rows, :] = points(cells[k], k)
    last = jnp.zeros((1, LANE), i32)
    lane_owner = jnp.zeros((1, LANE), i32)
    lane = lax.broadcasted_iota(i32, (1, LANE), 1)
    per_owner = p.blocks // p.cols
    to_scalar.wait()
    for k in range(p.cols):
        for m in range(per_owner):
            here = lane == k * per_owner + m
            last = jnp.where(here, blocks[k, 0, m], last)
            lane_owner = jnp.where(here, k, lane_owner)
    pencil, code = points(last, lane_owner)
    for k in range(p.halves):
        at = p.dests * p.halves + k
        pidx_v[pl.ds(at, 1), :] = pencil
        code_ref[pl.ds(at, 1), :] = code
    to_scalar = pltpu.make_async_copy(pidx_v, pidx, own_sem.at[6])

    def phases(i, carry):
        code = code_ref[pl.ds(i, 1), :]
        mirror = code >= p.code_rows
        kx = jnp.where(mirror, code - p.code_rows, code)
        span = lax.broadcasted_iota(i32, (p.code_rows, LANE), 0)
        hot = jnp.where((span == kx) | ((span == p.gx) & mirror), 1.0, 0.0).astype(bf16)
        phase = lax.dot_general(hot, xt_ref[...], (((0,), (0,)), ((), ())), preferred_element_type=f32)
        phase_ref[pl.ds(pl.multiple_of(i * LANE, LANE), LANE), :] = phase.astype(bf16)
        return carry

    groups = p.gy // p.group // p.steps

    def by_place(values):
        out = values[0]
        for o in range(1, p.outer):
            out = jnp.where(outer == o, values[o], out)
        return out

    order = [by_place([p.arrivals(o)[k] for o in range(p.outer)]) for k in range(p.outer)]

    def chunk(k):
        return k if p.merge > 1 else order[k]

    def z_step(stage, q, carry):
        lanes = pl.ds(pl.multiple_of(q * p.group_lanes, LANE), p.group_lanes)
        v = v_ref[:, :, lanes].astype(f32)
        parts = []
        for k in stage:
            size = p.merge * p.c_own
            c = c_ref[pl.ds(chunk(k) * size, size), :, lanes].astype(f32)
            parts += [v[i] * c[j] for j in range(size) for i in range(p.nv)]
            if LANE > p.lanes:
                parts.append(jnp.zeros((LANE - p.lanes, p.group_lanes), f32))
        prod = jnp.concatenate(parts, axis=0).astype(bf16)
        for t_ref, (start, width, ys) in zip(zt_refs, p.windows()):
            z = lax.dot_general(
                t_ref[...],
                prod[:, start : start + width],
                (((1,), (1,)), ((), ())),
                preferred_element_type=f32,
            )
            for n, k in enumerate(stage):
                for i, y in enumerate(ys):
                    base = (q * p.group + y) * p.zpitch
                    z_ref[chunk(k), pl.ds(base, p.zrows), :] = z[i * p.zrows : (i + 1) * p.zrows, n * LANE : (n + 1) * LANE]
        return carry

    def y_step(stage, kz, carry):
        cols = []
        for k in stage:
            parts = [z_ref[chunk(k), pl.ds(r * p.half + kz, p.gy, stride=p.zpitch), :] for r in range(2)]
            cols.append(jnp.concatenate(parts, axis=0).astype(bf16))
        out = jnp.dot(yt_ref[...], jnp.concatenate(cols, axis=1), preferred_element_type=f32)
        for s in range(2):
            for n, k in enumerate(stage):
                to = pl.ds(kz * (p.gy * p.pitch) + s * p.chunks + chunk(k), p.gy, stride=p.pitch)
                planes_ref[to, :] = out[s * p.gy : (s + 1) * p.gy, n * LANE : (n + 1) * LANE]
        return carry

    groups = p.gy // p.group // p.steps
    halves_all = (p.dests + 1) * p.halves
    stages = p.stages()
    cuts = [s[-1] + 1 if p.merge == 1 else p.outer for s in stages]

    def share(n, part, parts):
        return n * part // parts, n * (part + 1) // parts

    def looped(low, high, body, unroll):
        trips = (high - low) // unroll

        def several(i, carry):
            for u in range(unroll):
                body(low + i * unroll + u, carry)
            return carry

        if trips > 0:
            lax.fori_loop(0, trips, several, 0)
        for i in range(low + trips * unroll, high):
            body(i, 0)

    passed = 1
    for t, stage in enumerate(stages):
        until = p.outer - 1 if t == len(stages) - 1 else passed + 1
        for step in range(p.steps):
            if t == 0:
                looped(*share(halves_all, step, p.steps), phases, UNROLL_PHASE)
                if step == 0:
                    to_scalar.start()
            else:
                looped(*share(p.half, step, p.steps), functools.partial(y_step, stages[t - 1]), UNROLL_Y)
            for d in range(passed, until):
                pass_on(d, step)
            if t == 0:
                if step == 0:
                    for copy in local[:2]:
                        copy.wait()
                for d in range(1, p.inner):
                    v_copy(d, step).wait_recv()
            for d in range(max(1, cuts[t - 1] if t else 1), cuts[t]):
                wait_ends(d, step)
            looped(groups * step, groups * (step + 1), functools.partial(z_step, stage), UNROLL_Z)
        passed = until
    for d in range(1, p.inner):
        target = (outer * p.inner + lax.rem(inner + d, p.inner), col)
        pl.semaphore_signal(met, inc=1, device_id=target, device_id_type=MESH)
    to_scalar.wait()
    looped(0, p.half, functools.partial(y_step, stages[-1]), UNROLL_Y)
    if p.inner > 1:
        pl.semaphore_wait(met, p.inner - 1)

    def target_band(t):
        back = p.bands - 1 - t
        o = lax.rem(outer + lax.div(back, p.inner), p.outer)
        return o * p.inner + lax.rem(inner + lax.rem(back, p.inner), p.inner)

    def number(t, c):
        return lax.rem(col + 1 + c, p.cols) * p.bands + target_band(t)

    def pick(d, buf):
        at = d * p.halves
        for g in range(p.rows_dest):
            src = pidx[at + g // LANE, g % LANE]
            buf[pl.ds(g * p.pitch, p.tile), :] = planes_ref[pl.ds(src, p.tile), :]

    def turn(d, buf):
        rows = pl.ds(pl.multiple_of(d * p.rows_dest, LANE), p.rows_dest)
        cos = phase_ref[rows, :LANE].astype(f32)
        sin = phase_ref[rows, LANE : 2 * LANE].astype(f32)
        folded = 0.0
        for j in range(p.chunks):
            re = buf[pl.ds(j, p.rows_dest, stride=p.pitch), :]
            im = buf[pl.ds(p.chunks + j, p.rows_dest, stride=p.pitch), :]
            turned = jnp.concatenate([(cos * re - sin * im).astype(bf16), (sin * re + cos * im).astype(bf16)], axis=1)
            part = jnp.dot(turned, fold_ref[...], preferred_element_type=f32)
            folded = folded + (pltpu.roll(part, j * p.chunk_pairs, 1) if j else part)
        folded = folded * phase_ref[rows, 2 * LANE :].astype(f32)
        total = folded[: p.rows_packed]
        for q in range(1, p.pack):
            total = total + pltpu.roll(folded[q * p.rows_packed : (q + 1) * p.rows_packed], q * 2 * p.pairs, 1)
        part_ref[d] = total.astype(bf16)

    def peer(c):
        return (band, lax.rem(col + 1 + c, p.cols))

    def part_copy(t, c):
        return remote(part_ref.at[number(t, c)], row1.at[c, t], sem1.at[0, c, t], sem1.at[1, c, t], peer(c))

    def block_part_copy(c):
        src = part_ref.at[p.dests, pl.ds(0, p.block_rows)]
        return remote(src, block1.at[c], sem1.at[0, c, p.bands], sem1.at[1, c, p.bands], peer(c))

    def sum_copies(t):
        target = (target_band(t), col)
        return (
            remote(sum_ref.at[t], row_ref.at[band], sem2.at[0, 0, t], sem2.at[1, 0, t], target),
            remote(
                sum_ref.at[p.bands, pl.ds(0, p.block_rows)],
                block_ref.at[band],
                sem2.at[0, 1, t],
                sem2.at[1, 1, t],
                target,
            ),
        )

    def add_up(t):
        total = part_ref[number(t, p.cols - 1)].astype(f32)
        for c in range(p.cols - 1):
            part_copy(t, c).wait_recv()
        for c in range(p.cols - 1):
            total = total + row1[c, t].astype(f32)
        return total.astype(bf16)

    def add_up_block():
        total = part_ref[p.dests, : p.block_rows, :].astype(f32)
        for c in range(p.cols - 1):
            block_part_copy(c).wait_recv()
        for c in range(p.cols - 1):
            total = total + block1[c].astype(f32)
        return total.astype(bf16)

    def when(condition, action):
        pl.when(condition)(action)

    buffers = (pick_a, pick_b)
    pick(p.dests, pick_a)

    def send_sums(t):
        for copy in sum_copies(t):
            copy.start()

    def walk(t, carry):
        for c in range(p.cols):
            pick(number(t, c), buffers[(c + 1) % 2])
            if c == 0:
                turn(jnp.where(t == 0, p.dests, number(t - 1, p.cols - 1)), buffers[0])
                when(t > 0, lambda: part_copy(t - 1, p.cols - 2).start())
            else:
                turn(number(t, c - 1), buffers[c % 2])
                if c > 1:
                    part_copy(t, c - 2).start()
            if c == 1:
                when(t > 1, lambda: send_sums(t - 2))
            if c == min(2, p.cols - 1):

                @pl.when(t == 0)
                def _():
                    for k in range(p.cols - 1):
                        block_part_copy(k).start()

        @pl.when(t == 1)
        def _():
            sum_ref[p.bands, : p.block_rows, :] = add_up_block()

        @pl.when(t > 0)
        def _():
            sum_ref[t - 1] = add_up(t - 1)

        return carry

    lax.fori_loop(0, p.bands, walk, 0)
    last = p.bands - 1
    part_copy(last, p.cols - 2).start()
    turn(number(last, p.cols - 1), buffers[0])
    send_sums(last - 1)
    row_ref[band] = add_up(last)
    block_ref[band] = sum_ref[p.bands, : p.block_rows, :]

    for step in range(p.steps):
        for d in range(p.outer - 1):
            for way in range(2):

                @pl.when(passes(way, d))
                def _():
                    hop(way, d, step).wait_send()

        for d in range(1, p.inner):
            v_copy(d, step).wait_send()

    def close_parts(t, carry):
        for c in range(p.cols - 1):
            part_copy(t, c).wait_send()
        return carry

    lax.fori_loop(0, p.bands, close_parts, 0)
    for c in range(p.cols - 1):
        block_part_copy(c).wait_send()

    def close_sums(t, carry):
        for copy in sum_copies(t):
            copy.wait()
        return carry

    lax.fori_loop(0, p.bands - 1, close_sums, 0)

    pair_lane = lax.broadcasted_iota(i32, (1, LANE), 1)
    pair = lax.rem(pair_lane, p.pairs)
    pair_v, pair_c = lax.rem(pair, p.nv), lax.div(pair, p.nv)

    def spread(which, values):
        out = jnp.zeros((1, LANE), f32)
        for k, value in enumerate(values):
            out = jnp.where(which == k, value, out)
        return out

    valence = [energy_in[index_in[i]] for i in range(p.valences)]
    valence = [spread(pair_v, valence[o * p.nv : (o + 1) * p.nv]) for o in range(p.outer)]
    conduction = [
        spread(pair_c, [conduction_in[(o * p.inner + i) * p.c_own + l] for o in range(p.outer) for l in range(p.c_own)])
        for i in range(p.inner)
    ]
    norm = 1.0 / math.sqrt(p.valences * p.conductions)
    group_lanes = 2 * p.pairs
    acc = [jnp.zeros((p.rows_packed, 2 * p.freqs * p.blocks), f32) for _ in range(p.pack)]
    for b in range(p.bands):
        rows = row_ref[b]
        block = block_ref[b].astype(f32)[: p.blocks]
        first = jnp.where(pair_lane < group_lanes, block, 0.0)
        turned = jnp.where(
            pair_lane < p.pairs,
            -pltpu.roll(first, LANE - p.pairs, 1),
            jnp.where(pair_lane < group_lanes, pltpu.roll(first, p.pairs, 1), 0.0),
        )
        gap = conduction[b % p.inner] - valence[b // p.inner]
        parts = []
        for w in range(p.freqs):
            weight = -4.0 * gap / (gap * gap + freq_in[w] * freq_in[w]) * norm
            parts += [weight * first, weight * turned]
        right = jnp.concatenate(parts, axis=0)
        for q in range(p.pack):
            shifted = (pltpu.roll(right, q * group_lanes, 1) if q else right).astype(bf16)
            acc[q] = acc[q] + lax.dot_general(
                rows, shifted, (((1,), (1,)), ((), ())), preferred_element_type=f32
            )
    for q in range(p.pack):
        chi_ref[q * p.rows_packed : (q + 1) * p.rows_packed, :] = acc[q]


def run(p, index, energy, conduction, freq, v, c, cells, blocks):
    tables = p.z_tables() + [p.y_table(), p.fold_table()]
    vmem, hbm = pl.BlockSpec(memory_space=pltpu.VMEM), pl.BlockSpec(memory_space=pl.ANY)
    dma = pltpu.SemaphoreType.DMA
    f32, bf16, i32 = jnp.float32, jnp.bfloat16, jnp.int32
    halves_all = (p.dests + 1) * p.halves
    return pl.pallas_call(
        functools.partial(kernel, p),
        out_shape=jax.ShapeDtypeStruct((p.rows_dest, 2 * p.freqs * p.blocks), f32),
        in_specs=[pl.BlockSpec(memory_space=pltpu.SMEM)] * 4 + [hbm] * 5 + [vmem] * len(tables),
        out_specs=vmem,
        scratch_shapes=[
            pltpu.VMEM((p.chunks, (p.gy + 1) * p.zpitch, LANE), f32),
            pltpu.VMEM(((p.half * p.gy + 1) * p.pitch, LANE), f32),
            pltpu.VMEM(((p.rows_dest + 1) * p.pitch, LANE), f32),
            pltpu.VMEM(((p.rows_dest + 1) * p.pitch, LANE), f32),
            pltpu.VMEM((p.nv, p.slab_x, p.gy * p.gz), bf16),
            pltpu.VMEM((p.nc, p.slab_x, p.gy * p.gz), bf16),
            pltpu.VMEM((p.cols,) + cells.shape, i32),
            pltpu.VMEM((p.cols,) + blocks.shape, i32),
            pltpu.SMEM((p.cols,) + blocks.shape, i32),
            pltpu.VMEM((halves_all, LANE), i32),
            pltpu.SMEM((halves_all, LANE), i32),
            pltpu.VMEM((halves_all, LANE), i32),
            pltpu.VMEM((halves_all * LANE, p.wide), bf16),
            pltpu.VMEM((p.code_rows, p.wide), bf16),
            pltpu.VMEM((p.dests + 1, p.rows_packed, LANE), bf16),
            pltpu.VMEM((p.cols - 1, p.bands, p.rows_packed, LANE), bf16),
            pltpu.VMEM((p.bands + 1, p.rows_packed, LANE), bf16),
            pltpu.VMEM((p.bands, p.rows_packed, LANE), bf16),
            pltpu.VMEM((p.cols - 1, p.block_rows, LANE), bf16),
            pltpu.VMEM((p.bands, p.block_rows, LANE), bf16),
            dma((7,)),
            dma((p.inner - 1, p.steps)),
            dma((p.inner - 1, p.steps)),
            dma((2, p.outer - 1, p.steps)),
            dma((2, p.outer - 1, p.steps)),
            dma((2, 2, p.cols - 1)),
            dma((2, p.cols - 1, p.bands + 1)),
            dma((2, 2, p.bands)),
            pltpu.SemaphoreType.REGULAR,
        ],
        compiler_params=pltpu.CompilerParams(
            collective_id=0, has_side_effects=True, vmem_limit_bytes=VMEM_LIMIT
        ),
        name="chi",
    )(index, energy, conduction, freq, v, c, cells, blocks, p.x_tables(), *tables)


def per_device(
    valence_wave,
    conduction_wave,
    valence_index,
    occupied_energy,
    conduction_energy,
    frequency,
    gvec_cell,
    block_cell,
):
    cols, bands = lax.axis_size("col"), lax.axis_size("band")
    p = Plan(
        valence_wave.shape[0],
        conduction_wave.shape[0],
        valence_wave.shape[1],
        valence_wave.shape[2],
        cols,
        bands,
        gvec_cell.shape[0] * cols,
        block_cell.shape[0] * cols,
        frequency.shape[0],
    )
    return run(
        p,
        valence_index,
        occupied_energy,
        conduction_energy,
        frequency,
        valence_wave,
        conduction_wave,
        gvec_cell.reshape(-1, LANE),
        block_cell.reshape(1, -1),
    )


def solution(mesh):
    return jax.shard_map(
        per_device,
        mesh=mesh,
        in_specs=(
            P("band", "col", None),
            P("band", "col", None),
            P(),
            P(),
            P(),
            P(),
            P("col"),
            P("col"),
        ),
        out_specs=P(("col", "band"), None),
        check_vma=False,
    )
```

```python
import functools
import math

import jax
import jax.numpy as jnp
import numpy as np
from jax import lax
from jax.experimental import pallas as pl
from jax.experimental.pallas import tpu as pltpu
from jax.sharding import PartitionSpec as P

GY = 96
LANE = 128
SUB = 8
INNER = 2
STEPS = 8
UNROLL_PHASE = 4
UNROLL_Y = 7
UNROLL_Z = 3
MESH = pl.DeviceIdType.MESH
VMEM_LIMIT = 66_000_000


def up(n, k):
    return -(-n // k) * k


def rounded(a):
    return jnp.asarray(a, jnp.bfloat16)


def angles(rows, cols, length):
    return 2.0 * math.pi * ((np.outer(rows, cols) % length) / length)


class Plan:
    def __init__(self, v_own, c_own, slab_x, plane, cols, bands, rows_all, blocks_all, freqs):
        self.inner = INNER if bands % INNER == 0 else 1
        self.outer = bands // self.inner
        self.v_own, self.c_own = v_own, c_own
        self.nv, self.nc, self.slab_x = v_own * self.inner, c_own * self.outer, slab_x
        self.gy, self.gz, self.gx = GY, plane // GY, slab_x * cols
        self.cols, self.bands, self.freqs = cols, bands, freqs
        self.pairs = self.nv * self.nc
        self.merge = max(1, min(self.outer, LANE // (c_own * self.nv * slab_x)))
        if self.outer % self.merge:
            self.merge = 1
        self.chunks = self.outer // self.merge
        self.chunk_pairs = self.pairs // self.chunks
        self.lanes = self.chunk_pairs * slab_x
        self.tile = up(2 * self.chunks, SUB)
        self.pitch = self.tile + 1
        self.half = self.gz // 2 + 1
        self.zrows = up(2 * self.half, SUB)
        self.zpitch = self.zrows + 1
        self.group_lanes = self.gz * LANE // math.gcd(self.gz, LANE)
        self.group = self.group_lanes // self.gz
        self.dests = cols * bands
        self.rows_dest = rows_all // self.dests
        self.halves = self.rows_dest // LANE
        self.pack = LANE // (2 * self.pairs)
        self.rows_packed = self.rows_dest // self.pack
        self.cell_rows = rows_all // cols // LANE
        self.blocks = blocks_all
        self.block_rows = up(blocks_all, 2 * SUB)
        self.steps = STEPS
        self.code_rows = up(self.gx + 1, LANE)
        self.wide = 3 * LANE
        self.valences, self.conductions = v_own * bands, c_own * bands

    def stages(self):
        if self.merge > 1:
            return [list(range(self.chunks))]
        return [list(range(min(2, self.chunks)))] + [[k] for k in range(2, self.chunks)]

    def arrivals(self, at):
        return sorted(range(self.outer), key=lambda o: (abs(o - at), o))

    def windows(self):
        out, y = [], 0
        while y < self.group:
            start = y * self.gz // LANE * LANE
            ys = []
            while y < self.group and (y + 1) * self.gz <= start + 2 * LANE:
                ys.append(y)
                y += 1
            width = up(ys[-1] * self.gz + self.gz - start, LANE)
            out.append((start, width, ys))
        return out

    def z_tables(self):
        ang = angles(np.arange(self.half), np.arange(self.gz), self.gz)
        one = np.zeros((self.zrows, self.gz), np.float32)
        one[: self.half] = np.cos(ang)
        one[self.half : 2 * self.half] = -np.sin(ang)
        tables = []
        for start, width, ys in self.windows():
            t = np.zeros((len(ys) * self.zrows, width), np.float32)
            for i, y in enumerate(ys):
                lo = y * self.gz - start
                t[i * self.zrows : (i + 1) * self.zrows, lo : lo + self.gz] = one
            tables.append(rounded(t))
        return tables

    def y_table(self):
        ang = angles(np.arange(self.gy), np.arange(self.gy), self.gy)
        scale = 1.0 / math.sqrt(self.gy * self.gz)
        cos, sin = np.cos(ang) * scale, -np.sin(ang) * scale
        return rounded(np.block([[cos, -sin], [sin, cos]]))

    def x_tables(self):
        out = np.zeros((self.cols, self.code_rows, self.wide), np.float32)
        out[:, : self.gx, 2 * LANE :] = 1.0
        out[:, self.gx, 2 * LANE + self.pairs :] = -2.0
        scale = 1.0 / math.sqrt(self.gx)
        for col in range(self.cols):
            xs = col * self.slab_x + np.arange(self.lanes) % self.slab_x
            ang = angles(np.arange(self.gx), xs, self.gx)
            out[col, : self.gx, : self.lanes] = np.cos(ang) * scale
            out[col, : self.gx, LANE : LANE + self.lanes] = -np.sin(ang) * scale
        return rounded(out)

    def fold_table(self):
        out = np.zeros((2 * LANE, LANE), np.float32)
        n = np.arange(self.lanes)
        out[n, n // self.slab_x] = 1.0
        out[LANE + n, self.pairs + n // self.slab_x] = 1.0
        return rounded(out)


def place(p):
    band = lax.axis_index("band")
    return band // p.inner, lax.rem(band, p.inner)


def wrap(a, n):
    return jnp.where(a >= n, a - n, a)


def remote(src, dst, send, recv, target):
    return pltpu.make_async_remote_copy(src, dst, send, recv, device_id=target, device_id_type=MESH)


def kernel(p, index_in, energy_in, conduction_in, freq_in, v_in, c_in, cell_in, block_in, xt_in, *refs):
    n_win = len(p.windows())
    zt_in = refs[:n_win]
    yt_in, fold_in = refs[n_win : n_win + 2]
    refs = refs[n_win + 2 :]
    (chi_ref, *refs) = refs
    zt_refs = refs[:n_win]
    (yt_ref, fold_ref, index_ref, energy_ref, level_ref, freq_ref, z_ref, planes_ref, pick_a, pick_b, v_ref, c_ref, cells, blocks_v, blocks, pidx_v, pidx, code_ref,
     phase_ref, xt_ref, part_ref, row1, sum_ref, row_ref, block1, block_ref, own_sem, vs, vr, cs, cr, cell_sem, sem1, sem2, met, table_sem) = refs[n_win:]
    f32, bf16, i32 = jnp.float32, jnp.bfloat16, jnp.int32
    outer, inner = place(p)
    col, band = lax.axis_index("col"), lax.axis_index("band")
    line = [(outer > 0, outer - 1), (outer < p.outer - 1, outer + 1)]
    near = [(band, wrap(col + d, p.cols)) for d in range(1, p.cols)]
    near += [(outer * p.inner + wrap(inner + d, p.inner), col) for d in range(1, p.inner)]
    greeted = len(near) + sum(jnp.where(there, 1, 0) for there, _ in line)

    barrier = pltpu.get_barrier_semaphore()
    for target in near:
        pl.semaphore_signal(barrier, inc=1, device_id=target, device_id_type=MESH)
    for there, o in line:

        @pl.when(there)
        def _():
            pl.semaphore_signal(barrier, inc=1, device_id=(o * p.inner + inner, col), device_id_type=MESH)

    local = [
        pltpu.make_async_copy(v_in, v_ref.at[pl.ds(inner * p.v_own, p.v_own)], own_sem.at[0]),
        pltpu.make_async_copy(c_in, c_ref.at[pl.ds(outer * p.c_own, p.c_own)], own_sem.at[1]),
        pltpu.make_async_copy(cell_in, cells.at[col], own_sem.at[2]),
        pltpu.make_async_copy(xt_in.at[col], xt_ref, own_sem.at[3]),
        pltpu.make_async_copy(block_in, blocks_v.at[col], own_sem.at[4]),
    ]
    for copy in local:
        copy.start()
    tables = [*zip(zt_in, zt_refs), (yt_in, yt_ref), (fold_in, fold_ref), (index_in, index_ref)]
    tables += [(energy_in, energy_ref), (conduction_in, level_ref), (freq_in, freq_ref)]
    tables = [pltpu.make_async_copy(src, dst, table_sem.at[k]) for k, (src, dst) in enumerate(tables)]
    for copy in tables:
        copy.start()
    pl.semaphore_wait(barrier, greeted)

    step_lanes = p.gy * p.gz // p.steps

    def cut(ref, step):
        return ref.at[:, :, pl.ds(step * step_lanes, step_lanes)]

    def v_copy(d, step):
        slot = v_ref.at[pl.ds(inner * p.v_own, p.v_own)]
        target = (outer * p.inner + wrap(inner + d, p.inner), col)
        return remote(cut(v_in, step), cut(slot, step), vs.at[d - 1, step], vr.at[d - 1, step], target)

    def hop(way, d, step):
        slot = c_ref.at[pl.ds((outer - d if way == 0 else outer + d) * p.c_own, p.c_own)]
        target = ((outer + (1 if way == 0 else -1)) * p.inner + inner, col)
        src = c_in if d == 0 else slot
        return remote(cut(src, step), cut(slot, step), cs.at[way, d, step], cr.at[way, d, step], target)

    def arrives(way, d, step):
        slot = c_ref.at[pl.ds((outer - d if way == 0 else outer + d) * p.c_own, p.c_own)]
        return remote(cut(slot, step), cut(slot, step), cs.at[way, d - 1, step], cr.at[way, d - 1, step], (band, col))

    def passes(way, d):
        if way == 0:
            return (outer >= d) & (outer < p.outer - 1)
        return (outer + d < p.outer) & (outer > 0)

    def pass_on(d, step):
        for way in range(2):

            @pl.when(passes(way, d))
            def _():
                if d > 0:
                    arrives(way, d, step).wait_recv()
                hop(way, d, step).start()

    def wait_ends(d, step):
        @pl.when(outer == p.outer - 1)
        def _():
            arrives(0, d, step).wait_recv()

        @pl.when(outer == 0)
        def _():
            arrives(1, d, step).wait_recv()

    cell_copies = []
    for d in range(1, p.cols):
        target = (band, wrap(col + d, p.cols))
        cell_copies.append(remote(cell_in, cells.at[col], cell_sem.at[0, 0, d - 1], cell_sem.at[1, 0, d - 1], target))
        cell_copies.append(remote(block_in, blocks_v.at[col], cell_sem.at[0, 1, d - 1], cell_sem.at[1, 1, d - 1], target))
    for copy in cell_copies:
        copy.start()
    for step in range(p.steps):
        pass_on(0, step)
        for d in range(1, p.inner):
            v_copy(d, step).start()

    for copy in local[2:]:
        copy.wait()
    for copy in cell_copies:
        copy.wait()
    to_scalar = pltpu.make_async_copy(blocks_v, blocks, own_sem.at[5])
    to_scalar.start()
    slab_y = p.gy // p.cols

    def points(values, owner):
        def split(a, n):
            high = lax.div(a, jnp.full(a.shape, n, i32))
            return high, a - high * n

        kx, rest = split(values, slab_y * p.gz)
        ky, kz = split(rest, p.gz)
        ky = ky + owner * slab_y
        mirror = kz >= p.half
        kx = jnp.where(mirror & (kx > 0), p.gx - kx, kx)
        ky = jnp.where(mirror & (ky > 0), p.gy - ky, ky)
        kz = jnp.where(mirror, p.gz - kz, kz)
        return (kz * p.gy + ky) * p.pitch, kx + jnp.where(mirror, p.code_rows, 0)

    for k in range(p.cols):
        rows = pl.ds(k * p.cell_rows, p.cell_rows)
        pidx_v[rows, :], code_ref[rows, :] = points(cells[k], k)
    last = jnp.zeros((1, LANE), i32)
    lane_owner = jnp.zeros((1, LANE), i32)
    lane = lax.broadcasted_iota(i32, (1, LANE), 1)
    per_owner = p.blocks // p.cols
    to_scalar.wait()
    for k in range(p.cols):
        for m in range(per_owner):
            here = lane == k * per_owner + m
            last = jnp.where(here, blocks[k, 0, m], last)
            lane_owner = jnp.where(here, k, lane_owner)
    pencil, code = points(last, lane_owner)
    for k in range(p.halves):
        at = p.dests * p.halves + k
        pidx_v[pl.ds(at, 1), :] = pencil
        code_ref[pl.ds(at, 1), :] = code
    to_scalar = pltpu.make_async_copy(pidx_v, pidx, own_sem.at[6])

    def phases(i, carry):
        code = code_ref[pl.ds(i, 1), :]
        mirror = code >= p.code_rows
        kx = jnp.where(mirror, code - p.code_rows, code)
        span = lax.broadcasted_iota(i32, (p.code_rows, LANE), 0)
        hot = jnp.where((span == kx) | ((span == p.gx) & mirror), 1.0, 0.0).astype(bf16)
        phase = lax.dot_general(hot, xt_ref[...], (((0,), (0,)), ((), ())), preferred_element_type=f32)
        phase_ref[pl.ds(pl.multiple_of(i * LANE, LANE), LANE), :] = phase.astype(bf16)
        return carry

    groups = p.gy // p.group // p.steps

    def by_place(values):
        out = values[0]
        for o in range(1, p.outer):
            out = jnp.where(outer == o, values[o], out)
        return out

    order = [by_place([p.arrivals(o)[k] for o in range(p.outer)]) for k in range(p.outer)]

    def chunk(k):
        return k if p.merge > 1 else order[k]

    def z_step(stage, q, carry):
        lanes = pl.ds(pl.multiple_of(q * p.group_lanes, LANE), p.group_lanes)
        v = v_ref[:, :, lanes].astype(f32)
        parts = []
        for k in stage:
            size = p.merge * p.c_own
            c = c_ref[pl.ds(chunk(k) * size, size), :, lanes].astype(f32)
            parts += [v[i] * c[j] for j in range(size) for i in range(p.nv)]
            if LANE > p.lanes:
                parts.append(jnp.zeros((LANE - p.lanes, p.group_lanes), f32))
        prod = jnp.concatenate(parts, axis=0).astype(bf16)
        for t_ref, (start, width, ys) in zip(zt_refs, p.windows()):
            z = lax.dot_general(
                t_ref[...],
                prod[:, start : start + width],
                (((1,), (1,)), ((), ())),
                preferred_element_type=f32,
            )
            for n, k in enumerate(stage):
                for i, y in enumerate(ys):
                    base = (q * p.group + y) * p.zpitch
                    z_ref[chunk(k), pl.ds(base, p.zrows), :] = z[i * p.zrows : (i + 1) * p.zrows, n * LANE : (n + 1) * LANE]
        return carry

    def y_step(stage, kz, carry):
        cols = []
        for k in stage:
            parts = [z_ref[chunk(k), pl.ds(r * p.half + kz, p.gy, stride=p.zpitch), :] for r in range(2)]
            cols.append(jnp.concatenate(parts, axis=0).astype(bf16))
        out = jnp.dot(yt_ref[...], jnp.concatenate(cols, axis=1), preferred_element_type=f32)
        for s in range(2):
            for n, k in enumerate(stage):
                to = pl.ds(kz * (p.gy * p.pitch) + s * p.chunks + chunk(k), p.gy, stride=p.pitch)
                planes_ref[to, :] = out[s * p.gy : (s + 1) * p.gy, n * LANE : (n + 1) * LANE]
        return carry

    groups = p.gy // p.group // p.steps
    halves_all = (p.dests + 1) * p.halves
    stages = p.stages()
    cuts = [s[-1] + 1 if p.merge == 1 else p.outer for s in stages]

    def share(n, part, parts):
        return n * part // parts, n * (part + 1) // parts

    def looped(low, high, body, unroll):
        trips = (high - low) // unroll

        def several(i, carry):
            for u in range(unroll):
                body(low + i * unroll + u, carry)
            return carry

        if trips > 0:
            lax.fori_loop(0, trips, several, 0)
        for i in range(low + trips * unroll, high):
            body(i, 0)

    passed = 1
    for t, stage in enumerate(stages):
        until = p.outer - 1 if t == len(stages) - 1 else passed + 1
        for step in range(p.steps):
            if t == 0:
                looped(*share(halves_all, step, p.steps), phases, UNROLL_PHASE)
                if step == 0:
                    to_scalar.start()
            else:
                looped(*share(p.half, step, p.steps), functools.partial(y_step, stages[t - 1]), UNROLL_Y)
            for d in range(passed, until):
                pass_on(d, step)
            if t == 0:
                if step == 0:
                    for copy in local[:2] + tables:
                        copy.wait()
                for d in range(1, p.inner):
                    v_copy(d, step).wait_recv()
            for d in range(max(1, cuts[t - 1] if t else 1), cuts[t]):
                wait_ends(d, step)
            looped(groups * step, groups * (step + 1), functools.partial(z_step, stage), UNROLL_Z)
        passed = until
    for d in range(1, p.inner):
        target = (outer * p.inner + wrap(inner + d, p.inner), col)
        pl.semaphore_signal(met, inc=1, device_id=target, device_id_type=MESH)
    to_scalar.wait()
    looped(0, p.half, functools.partial(y_step, stages[-1]), UNROLL_Y)
    if p.inner > 1:
        pl.semaphore_wait(met, p.inner - 1)

    def target_band(t):
        back = p.bands - 1 - t
        high = (back * (65536 // p.inner + 1)) >> 16
        return wrap(outer + high, p.outer) * p.inner + wrap(inner + back - high * p.inner, p.inner)

    peers = [wrap(col + 1 + c, p.cols) for c in range(p.cols)]

    def number(t, c):
        return peers[c] * p.bands + target_band(t)

    def pick(d, buf):
        at = d * p.halves
        for g in range(p.rows_dest):
            src = pidx[at + g // LANE, g % LANE]
            buf[pl.ds(g * p.pitch, p.tile), :] = planes_ref[pl.ds(src, p.tile), :]

    def turn(d, buf):
        rows = pl.ds(pl.multiple_of(d * p.rows_dest, LANE), p.rows_dest)
        cos = phase_ref[rows, :LANE].astype(f32)
        sin = phase_ref[rows, LANE : 2 * LANE].astype(f32)
        folded = 0.0
        for j in range(p.chunks):
            re = buf[pl.ds(j, p.rows_dest, stride=p.pitch), :]
            im = buf[pl.ds(p.chunks + j, p.rows_dest, stride=p.pitch), :]
            turned = jnp.concatenate([(cos * re - sin * im).astype(bf16), (sin * re + cos * im).astype(bf16)], axis=1)
            part = jnp.dot(turned, fold_ref[...], preferred_element_type=f32)
            folded = folded + (pltpu.roll(part, j * p.chunk_pairs, 1) if j else part)
        folded = folded * phase_ref[rows, 2 * LANE :].astype(f32)
        total = folded[: p.rows_packed]
        for q in range(1, p.pack):
            total = total + pltpu.roll(folded[q * p.rows_packed : (q + 1) * p.rows_packed], q * 2 * p.pairs, 1)
        part_ref[d] = total.astype(bf16)

    def peer(c):
        return (band, peers[c])

    def part_copy(t, c):
        return remote(part_ref.at[number(t, c)], row1.at[c, t], sem1.at[0, c, t], sem1.at[1, c, t], peer(c))

    def block_part_copy(c):
        src = part_ref.at[p.dests, pl.ds(0, p.block_rows)]
        return remote(src, block1.at[c], sem1.at[0, c, p.bands], sem1.at[1, c, p.bands], peer(c))

    def sum_copies(t):
        target = (target_band(t), col)
        return (
            remote(sum_ref.at[t], row_ref.at[band], sem2.at[0, 0, t], sem2.at[1, 0, t], target),
            remote(
                sum_ref.at[p.bands, pl.ds(0, p.block_rows)],
                block_ref.at[band],
                sem2.at[0, 1, t],
                sem2.at[1, 1, t],
                target,
            ),
        )

    def add_up(t):
        total = part_ref[number(t, p.cols - 1)].astype(f32)
        for c in range(p.cols - 1):
            part_copy(t, c).wait_recv()
        for c in range(p.cols - 1):
            total = total + row1[c, t].astype(f32)
        return total.astype(bf16)

    def add_up_block():
        total = part_ref[p.dests, : p.block_rows, :].astype(f32)
        for c in range(p.cols - 1):
            block_part_copy(c).wait_recv()
        for c in range(p.cols - 1):
            total = total + block1[c].astype(f32)
        return total.astype(bf16)

    def when(condition, action):
        pl.when(condition)(action)

    buffers = (pick_a, pick_b)
    pick(p.dests, pick_a)

    def send_sums(t):
        for copy in sum_copies(t):
            copy.start()

    def walk(t, carry):
        for c in range(p.cols):
            pick(number(t, c), buffers[(c + 1) % 2])
            if c == 0:
                turn(jnp.where(t == 0, p.dests, number(t - 1, p.cols - 1)), buffers[0])
                when(t > 0, lambda: part_copy(t - 1, p.cols - 2).start())
            else:
                turn(number(t, c - 1), buffers[c % 2])
                if c > 1:
                    part_copy(t, c - 2).start()
            if c == 1:
                when(t > 2, lambda: send_sums(t - 3))
            if c == min(2, p.cols - 1):

                @pl.when(t == 0)
                def _():
                    for k in range(p.cols - 1):
                        block_part_copy(k).start()

        @pl.when(t == 1)
        def _():
            sum_ref[p.bands, : p.block_rows, :] = add_up_block()

        @pl.when(t > 1)
        def _():
            sum_ref[t - 2] = add_up(t - 2)

        return carry

    lax.fori_loop(0, p.bands, walk, 0)
    last = p.bands - 1
    part_copy(last, p.cols - 2).start()
    sum_ref[last - 1] = add_up(last - 1)
    turn(number(last, p.cols - 1), buffers[0])
    send_sums(last - 2)
    send_sums(last - 1)
    row_ref[band] = add_up(last)
    block_ref[band] = sum_ref[p.bands, : p.block_rows, :]

    for step in range(p.steps):
        for d in range(p.outer - 1):
            for way in range(2):

                @pl.when(passes(way, d))
                def _():
                    hop(way, d, step).wait_send()

        for d in range(1, p.inner):
            v_copy(d, step).wait_send()

    def close_parts(t, carry):
        for c in range(p.cols - 1):
            part_copy(t, c).wait_send()
        return carry

    lax.fori_loop(0, p.bands, close_parts, 0)
    for c in range(p.cols - 1):
        block_part_copy(c).wait_send()

    def close_sums(t, carry):
        for copy in sum_copies(t):
            copy.wait()
        return carry

    lax.fori_loop(0, p.bands - 1, close_sums, 0)

    pair_lane = lax.broadcasted_iota(i32, (1, LANE), 1)
    pair = lax.rem(pair_lane, p.pairs)
    pair_v, pair_c = lax.rem(pair, p.nv), lax.div(pair, p.nv)

    def spread(which, values):
        out = jnp.zeros((1, LANE), f32)
        for k, value in enumerate(values):
            out = jnp.where(which == k, value, out)
        return out

    valence = [energy_ref[index_ref[i]] for i in range(p.valences)]
    valence = [spread(pair_v, valence[o * p.nv : (o + 1) * p.nv]) for o in range(p.outer)]
    conduction = [
        spread(pair_c, [level_ref[(o * p.inner + i) * p.c_own + l] for o in range(p.outer) for l in range(p.c_own)])
        for i in range(p.inner)
    ]
    norm = 1.0 / math.sqrt(p.valences * p.conductions)
    group_lanes = 2 * p.pairs
    acc = [jnp.zeros((p.rows_packed, 2 * p.freqs * p.blocks), f32) for _ in range(p.pack)]
    for b in range(p.bands):
        rows = row_ref[b]
        block = block_ref[b].astype(f32)[: p.blocks]
        first = jnp.where(pair_lane < group_lanes, block, 0.0)
        turned = jnp.where(
            pair_lane < p.pairs,
            -pltpu.roll(first, LANE - p.pairs, 1),
            jnp.where(pair_lane < group_lanes, pltpu.roll(first, p.pairs, 1), 0.0),
        )
        gap = conduction[b % p.inner] - valence[b // p.inner]
        parts = []
        for w in range(p.freqs):
            weight = -4.0 * gap / (gap * gap + freq_ref[w] * freq_ref[w]) * norm
            parts += [weight * first, weight * turned]
        right = jnp.concatenate(parts, axis=0)
        for q in range(p.pack):
            shifted = (pltpu.roll(right, q * group_lanes, 1) if q else right).astype(bf16)
            acc[q] = acc[q] + lax.dot_general(
                rows, shifted, (((1,), (1,)), ((), ())), preferred_element_type=f32
            )
    for q in range(p.pack):
        chi_ref[q * p.rows_packed : (q + 1) * p.rows_packed, :] = acc[q]


def run(p, index, energy, conduction, freq, v, c, cells, blocks):
    tables = p.z_tables() + [p.y_table(), p.fold_table()]
    vmem, hbm = pl.BlockSpec(memory_space=pltpu.VMEM), pl.BlockSpec(memory_space=pl.ANY)
    dma = pltpu.SemaphoreType.DMA
    f32, bf16, i32 = jnp.float32, jnp.bfloat16, jnp.int32
    halves_all = (p.dests + 1) * p.halves
    return pl.pallas_call(
        functools.partial(kernel, p),
        out_shape=jax.ShapeDtypeStruct((p.rows_dest, 2 * p.freqs * p.blocks), f32),
        in_specs=[hbm] * (9 + len(tables)),
        out_specs=vmem,
        scratch_shapes=[pltpu.VMEM(t.shape, bf16) for t in tables]
        + [pltpu.SMEM(a.shape, a.dtype) for a in (index, energy, conduction, freq)]
        + [
            pltpu.VMEM((p.chunks, (p.gy + 1) * p.zpitch, LANE), f32),
            pltpu.VMEM(((p.half * p.gy + 1) * p.pitch, LANE), f32),
            pltpu.VMEM(((p.rows_dest + 1) * p.pitch, LANE), f32),
            pltpu.VMEM(((p.rows_dest + 1) * p.pitch, LANE), f32),
            pltpu.VMEM((p.nv, p.slab_x, p.gy * p.gz), bf16),
            pltpu.VMEM((p.nc, p.slab_x, p.gy * p.gz), bf16),
            pltpu.VMEM((p.cols,) + cells.shape, i32),
            pltpu.VMEM((p.cols,) + blocks.shape, i32),
            pltpu.SMEM((p.cols,) + blocks.shape, i32),
            pltpu.VMEM((halves_all, LANE), i32),
            pltpu.SMEM((halves_all, LANE), i32),
            pltpu.VMEM((halves_all, LANE), i32),
            pltpu.VMEM((halves_all * LANE, p.wide), bf16),
            pltpu.VMEM((p.code_rows, p.wide), bf16),
            pltpu.VMEM((p.dests + 1, p.rows_packed, LANE), bf16),
            pltpu.VMEM((p.cols - 1, p.bands, p.rows_packed, LANE), bf16),
            pltpu.VMEM((p.bands + 1, p.rows_packed, LANE), bf16),
            pltpu.VMEM((p.bands, p.rows_packed, LANE), bf16),
            pltpu.VMEM((p.cols - 1, p.block_rows, LANE), bf16),
            pltpu.VMEM((p.bands, p.block_rows, LANE), bf16),
            dma((7,)),
            dma((p.inner - 1, p.steps)),
            dma((p.inner - 1, p.steps)),
            dma((2, p.outer - 1, p.steps)),
            dma((2, p.outer - 1, p.steps)),
            dma((2, 2, p.cols - 1)),
            dma((2, p.cols - 1, p.bands + 1)),
            dma((2, 2, p.bands)),
            pltpu.SemaphoreType.REGULAR,
            dma((len(tables) + 4,)),
        ],
        compiler_params=pltpu.CompilerParams(
            collective_id=0, has_side_effects=True, vmem_limit_bytes=VMEM_LIMIT
        ),
        name="chi",
    )(index, energy, conduction, freq, v, c, cells, blocks, p.x_tables(), *tables)


def per_device(
    valence_wave,
    conduction_wave,
    valence_index,
    occupied_energy,
    conduction_energy,
    frequency,
    gvec_cell,
    block_cell,
):
    cols, bands = lax.axis_size("col"), lax.axis_size("band")
    p = Plan(
        valence_wave.shape[0],
        conduction_wave.shape[0],
        valence_wave.shape[1],
        valence_wave.shape[2],
        cols,
        bands,
        gvec_cell.shape[0] * cols,
        block_cell.shape[0] * cols,
        frequency.shape[0],
    )
    return run(
        p,
        valence_index,
        occupied_energy,
        conduction_energy,
        frequency,
        valence_wave,
        conduction_wave,
        gvec_cell.reshape(-1, LANE),
        block_cell.reshape(1, -1),
    )


def solution(mesh):
    return jax.shard_map(
        per_device,
        mesh=mesh,
        in_specs=(
            P("band", "col", None),
            P("band", "col", None),
            P(),
            P(),
            P(),
            P(),
            P("col"),
            P("col"),
        ),
        out_specs=P(("col", "band"), None),
        check_vma=False,
    )
```

```python
import functools
import math

import jax
import jax.numpy as jnp
import numpy as np
from jax import lax
from jax.experimental import pallas as pl
from jax.experimental.pallas import tpu as pltpu
from jax.sharding import PartitionSpec as P

GY = 96
LANE = 128
SUB = 8
INNER = 2
STEPS = 8
UNROLL_PHASE = 4
UNROLL_Y = 7
UNROLL_Z = 3
MESH = pl.DeviceIdType.MESH
VMEM_LIMIT = 66_000_000


def up(n, k):
    return -(-n // k) * k


def rounded(a):
    return jnp.asarray(a, jnp.bfloat16)


def angles(rows, cols, length):
    return 2.0 * math.pi * ((np.outer(rows, cols) % length) / length)


class Plan:
    def __init__(self, v_own, c_own, slab_x, plane, cols, bands, rows_all, blocks_all, freqs):
        self.inner = INNER if bands % INNER == 0 else 1
        self.outer = bands // self.inner
        self.v_own, self.c_own = v_own, c_own
        self.nv, self.nc, self.slab_x = v_own * self.inner, c_own * self.outer, slab_x
        self.gy, self.gz, self.gx = GY, plane // GY, slab_x * cols
        self.cols, self.bands, self.freqs = cols, bands, freqs
        self.pairs = self.nv * self.nc
        self.merge = max(1, min(self.outer, LANE // (c_own * self.nv * slab_x)))
        if self.outer % self.merge:
            self.merge = 1
        self.chunks = self.outer // self.merge
        self.chunk_pairs = self.pairs // self.chunks
        self.lanes = self.chunk_pairs * slab_x
        self.tile = up(2 * self.chunks, SUB)
        self.pitch = self.tile + 1
        self.half = self.gz // 2 + 1
        self.zrows = up(2 * self.half, SUB)
        self.zpitch = self.zrows + 1
        self.group_lanes = self.gz * LANE // math.gcd(self.gz, LANE)
        self.group = self.group_lanes // self.gz
        self.dests = cols * bands
        self.rows_dest = rows_all // self.dests
        self.halves = self.rows_dest // LANE
        self.pack = LANE // (2 * self.pairs)
        self.rows_packed = self.rows_dest // self.pack
        self.cell_rows = rows_all // cols // LANE
        self.blocks = blocks_all
        self.block_rows = up(blocks_all, 2 * SUB)
        self.steps = STEPS
        self.code_rows = up(self.gx + 1, LANE)
        self.wide = 3 * LANE
        self.valences, self.conductions = v_own * bands, c_own * bands

    def stages(self):
        if self.merge > 1:
            return [list(range(self.chunks))]
        return [list(range(min(2, self.chunks)))] + [[k] for k in range(2, self.chunks)]

    def arrivals(self, at):
        return sorted(range(self.outer), key=lambda o: (abs(o - at), o))

    def windows(self):
        out, y = [], 0
        while y < self.group:
            start = y * self.gz // LANE * LANE
            ys = []
            while y < self.group and (y + 1) * self.gz <= start + 2 * LANE:
                ys.append(y)
                y += 1
            width = up(ys[-1] * self.gz + self.gz - start, LANE)
            out.append((start, width, ys))
        return out

    def z_tables(self):
        ang = angles(np.arange(self.half), np.arange(self.gz), self.gz)
        one = np.zeros((self.zrows, self.gz), np.float32)
        one[: self.half] = np.cos(ang)
        one[self.half : 2 * self.half] = -np.sin(ang)
        tables = []
        for start, width, ys in self.windows():
            t = np.zeros((len(ys) * self.zrows, width), np.float32)
            for i, y in enumerate(ys):
                lo = y * self.gz - start
                t[i * self.zrows : (i + 1) * self.zrows, lo : lo + self.gz] = one
            tables.append(rounded(t))
        return tables

    def y_table(self):
        ang = angles(np.arange(self.gy), np.arange(self.gy), self.gy)
        scale = 1.0 / math.sqrt(self.gy * self.gz)
        cos, sin = np.cos(ang) * scale, -np.sin(ang) * scale
        return rounded(np.block([[cos, -sin], [sin, cos]]))

    def x_tables(self):
        out = np.zeros((self.cols, self.code_rows, self.wide), np.float32)
        out[:, : self.gx, 2 * LANE :] = 1.0
        out[:, self.gx, 2 * LANE + self.pairs :] = -2.0
        scale = 1.0 / math.sqrt(self.gx)
        for col in range(self.cols):
            xs = col * self.slab_x + np.arange(self.lanes) % self.slab_x
            ang = angles(np.arange(self.gx), xs, self.gx)
            out[col, : self.gx, : self.lanes] = np.cos(ang) * scale
            out[col, : self.gx, LANE : LANE + self.lanes] = -np.sin(ang) * scale
        return rounded(out)

    def fold_table(self):
        out = np.zeros((2 * LANE, LANE), np.float32)
        n = np.arange(self.lanes)
        out[n, n // self.slab_x] = 1.0
        out[LANE + n, self.pairs + n // self.slab_x] = 1.0
        return rounded(out)


def place(p):
    band = lax.axis_index("band")
    return band // p.inner, lax.rem(band, p.inner)


def wrap(a, n):
    return jnp.where(a >= n, a - n, a)


def remote(src, dst, send, recv, target):
    return pltpu.make_async_remote_copy(src, dst, send, recv, device_id=target, device_id_type=MESH)


def kernel(p, index_in, energy_in, conduction_in, freq_in, v_in, c_in, cell_in, block_in, xt_in, *refs):
    n_win = len(p.windows())
    zt_in = refs[:n_win]
    yt_in, fold_in = refs[n_win : n_win + 2]
    refs = refs[n_win + 2 :]
    (chi_ref, *refs) = refs
    zt_refs = refs[:n_win]
    (yt_ref, fold_ref, index_ref, energy_ref, level_ref, freq_ref, z_ref, planes_ref, pick_a, pick_b, v_ref, c_ref, cells, blocks_v, blocks, pidx_v, pidx, code_ref,
     phase_ref, xt_ref, part_ref, row1, sum_ref, row_ref, block1, block_ref, own_sem, vs, vr, cs, cr, cell_sem, sem1, sem2, met, table_sem) = refs[n_win:]
    f32, bf16, i32 = jnp.float32, jnp.bfloat16, jnp.int32
    outer, inner = place(p)
    col, band = lax.axis_index("col"), lax.axis_index("band")
    line = [(outer > 0, outer - 1), (outer < p.outer - 1, outer + 1)]
    near = [(band, wrap(col + d, p.cols)) for d in range(1, p.cols)]
    near += [(outer * p.inner + wrap(inner + d, p.inner), col) for d in range(1, p.inner)]
    greeted = len(near) + sum(jnp.where(there, 1, 0) for there, _ in line)

    barrier = pltpu.get_barrier_semaphore()
    for target in near:
        pl.semaphore_signal(barrier, inc=1, device_id=target, device_id_type=MESH)
    for there, o in line:

        @pl.when(there)
        def _():
            pl.semaphore_signal(barrier, inc=1, device_id=(o * p.inner + inner, col), device_id_type=MESH)

    local = [
        pltpu.make_async_copy(v_in, v_ref.at[pl.ds(inner * p.v_own, p.v_own)], own_sem.at[0]),
        pltpu.make_async_copy(c_in, c_ref.at[pl.ds(outer * p.c_own, p.c_own)], own_sem.at[1]),
        pltpu.make_async_copy(cell_in, cells.at[col], own_sem.at[2]),
        pltpu.make_async_copy(xt_in.at[col], xt_ref, own_sem.at[3]),
        pltpu.make_async_copy(block_in, blocks_v.at[col], own_sem.at[4]),
    ]
    for copy in local:
        copy.start()
    tables = [*zip(zt_in, zt_refs), (yt_in, yt_ref), (fold_in, fold_ref), (index_in, index_ref)]
    tables += [(energy_in, energy_ref), (conduction_in, level_ref), (freq_in, freq_ref)]
    tables = [pltpu.make_async_copy(src, dst, table_sem.at[k]) for k, (src, dst) in enumerate(tables)]
    for copy in tables:
        copy.start()
    pl.semaphore_wait(barrier, greeted)

    step_lanes = p.gy * p.gz // p.steps

    def cut(ref, step):
        return ref.at[:, :, pl.ds(step * step_lanes, step_lanes)]

    def v_copy(d, step):
        slot = v_ref.at[pl.ds(inner * p.v_own, p.v_own)]
        target = (outer * p.inner + wrap(inner + d, p.inner), col)
        return remote(cut(v_in, step), cut(slot, step), vs.at[d - 1, step], vr.at[d - 1, step], target)

    def hop(way, d, step):
        slot = c_ref.at[pl.ds((outer - d if way == 0 else outer + d) * p.c_own, p.c_own)]
        target = ((outer + (1 if way == 0 else -1)) * p.inner + inner, col)
        src = c_in if d == 0 else slot
        return remote(cut(src, step), cut(slot, step), cs.at[way, d, step], cr.at[way, d, step], target)

    def arrives(way, d, step):
        slot = c_ref.at[pl.ds((outer - d if way == 0 else outer + d) * p.c_own, p.c_own)]
        return remote(cut(slot, step), cut(slot, step), cs.at[way, d - 1, step], cr.at[way, d - 1, step], (band, col))

    def passes(way, d):
        if way == 0:
            return (outer >= d) & (outer < p.outer - 1)
        return (outer + d < p.outer) & (outer > 0)

    def pass_on(d, step):
        for way in range(2):

            @pl.when(passes(way, d))
            def _():
                if d > 0:
                    arrives(way, d, step).wait_recv()
                hop(way, d, step).start()

    def wait_ends(d, step):
        @pl.when(outer == p.outer - 1)
        def _():
            arrives(0, d, step).wait_recv()

        @pl.when(outer == 0)
        def _():
            arrives(1, d, step).wait_recv()

    cell_copies = []
    for d in range(1, p.cols):
        target = (band, wrap(col + d, p.cols))
        cell_copies.append(remote(cell_in, cells.at[col], cell_sem.at[0, 0, d - 1], cell_sem.at[1, 0, d - 1], target))
        cell_copies.append(remote(block_in, blocks_v.at[col], cell_sem.at[0, 1, d - 1], cell_sem.at[1, 1, d - 1], target))
    for copy in cell_copies:
        copy.start()
    for step in range(p.steps):
        pass_on(0, step)
        for d in range(1, p.inner):
            v_copy(d, step).start()

    for copy in local[2:]:
        copy.wait()
    for copy in cell_copies:
        copy.wait()
    to_scalar = pltpu.make_async_copy(blocks_v, blocks, own_sem.at[5])
    to_scalar.start()
    slab_y = p.gy // p.cols

    def points(values, owner):
        def split(a, n):
            high = lax.div(a, jnp.full(a.shape, n, i32))
            return high, a - high * n

        kx, rest = split(values, slab_y * p.gz)
        ky, kz = split(rest, p.gz)
        ky = ky + owner * slab_y
        mirror = kz >= p.half
        kx = jnp.where(mirror & (kx > 0), p.gx - kx, kx)
        ky = jnp.where(mirror & (ky > 0), p.gy - ky, ky)
        kz = jnp.where(mirror, p.gz - kz, kz)
        return (kz * p.gy + ky) * p.pitch, kx + jnp.where(mirror, p.code_rows, 0)

    for k in range(p.cols):
        rows = pl.ds(k * p.cell_rows, p.cell_rows)
        pidx_v[rows, :], code_ref[rows, :] = points(cells[k], k)
    last = jnp.zeros((1, LANE), i32)
    lane_owner = jnp.zeros((1, LANE), i32)
    lane = lax.broadcasted_iota(i32, (1, LANE), 1)
    per_owner = p.blocks // p.cols
    to_scalar.wait()
    for k in range(p.cols):
        for m in range(per_owner):
            here = lane == k * per_owner + m
            last = jnp.where(here, blocks[k, 0, m], last)
            lane_owner = jnp.where(here, k, lane_owner)
    pencil, code = points(last, lane_owner)
    for k in range(p.halves):
        at = p.dests * p.halves + k
        pidx_v[pl.ds(at, 1), :] = pencil
        code_ref[pl.ds(at, 1), :] = code
    to_scalar = pltpu.make_async_copy(pidx_v, pidx, own_sem.at[6])

    def phases(i, carry):
        code = code_ref[pl.ds(i, 1), :]
        mirror = code >= p.code_rows
        kx = jnp.where(mirror, code - p.code_rows, code)
        span = lax.broadcasted_iota(i32, (p.code_rows, LANE), 0)
        hot = jnp.where((span == kx) | ((span == p.gx) & mirror), 1.0, 0.0).astype(bf16)
        phase = lax.dot_general(hot, xt_ref[...], (((0,), (0,)), ((), ())), preferred_element_type=f32)
        phase_ref[pl.ds(pl.multiple_of(i * LANE, LANE), LANE), :] = phase.astype(bf16)
        return carry

    groups = p.gy // p.group // p.steps

    def by_place(values):
        out = values[0]
        for o in range(1, p.outer):
            out = jnp.where(outer == o, values[o], out)
        return out

    order = [by_place([p.arrivals(o)[k] for o in range(p.outer)]) for k in range(p.outer)]

    def chunk(k):
        return k if p.merge > 1 else order[k]

    def z_step(stage, q, carry):
        lanes = pl.ds(pl.multiple_of(q * p.group_lanes, LANE), p.group_lanes)
        v = v_ref[:, :, lanes].astype(f32)
        parts = []
        for k in stage:
            size = p.merge * p.c_own
            c = c_ref[pl.ds(chunk(k) * size, size), :, lanes].astype(f32)
            parts += [v[i] * c[j] for j in range(size) for i in range(p.nv)]
            if LANE > p.lanes:
                parts.append(jnp.zeros((LANE - p.lanes, p.group_lanes), f32))
        prod = jnp.concatenate(parts, axis=0).astype(bf16)
        for t_ref, (start, width, ys) in zip(zt_refs, p.windows()):
            z = lax.dot_general(
                t_ref[...],
                prod[:, start : start + width],
                (((1,), (1,)), ((), ())),
                preferred_element_type=f32,
            )
            for n, k in enumerate(stage):
                for i, y in enumerate(ys):
                    base = (q * p.group + y) * p.zpitch
                    z_ref[chunk(k), pl.ds(base, p.zrows), :] = z[i * p.zrows : (i + 1) * p.zrows, n * LANE : (n + 1) * LANE]
        return carry

    def y_step(stage, kz, carry):
        cols = []
        for k in stage:
            parts = [z_ref[chunk(k), pl.ds(r * p.half + kz, p.gy, stride=p.zpitch), :] for r in range(2)]
            cols.append(jnp.concatenate(parts, axis=0).astype(bf16))
        out = jnp.dot(yt_ref[...], jnp.concatenate(cols, axis=1), preferred_element_type=f32)
        for s in range(2):
            for n, k in enumerate(stage):
                to = pl.ds(kz * (p.gy * p.pitch) + s * p.chunks + chunk(k), p.gy, stride=p.pitch)
                planes_ref[to, :] = out[s * p.gy : (s + 1) * p.gy, n * LANE : (n + 1) * LANE]
        return carry

    groups = p.gy // p.group // p.steps
    halves_all = (p.dests + 1) * p.halves
    stages = p.stages()
    cuts = [s[-1] + 1 if p.merge == 1 else p.outer for s in stages]

    def share(n, part, parts):
        return n * part // parts, n * (part + 1) // parts

    def looped(low, high, body, unroll):
        trips = (high - low) // unroll

        def several(i, carry):
            for u in range(unroll):
                body(low + i * unroll + u, carry)
            return carry

        if trips > 0:
            lax.fori_loop(0, trips, several, 0)
        for i in range(low + trips * unroll, high):
            body(i, 0)

    passed = 1
    for t, stage in enumerate(stages):
        until = p.outer - 1 if t == len(stages) - 1 else passed + 1
        for step in range(p.steps):
            if t == 0:
                looped(*share(halves_all, step, p.steps), phases, UNROLL_PHASE)
                if step == 0:
                    to_scalar.start()
            else:
                looped(*share(p.half, step, p.steps), functools.partial(y_step, stages[t - 1]), UNROLL_Y)
            for d in range(passed, until):
                pass_on(d, step)
            if t == 0:
                if step == 0:
                    for copy in local[:2] + tables:
                        copy.wait()
                for d in range(1, p.inner):
                    v_copy(d, step).wait_recv()
            for d in range(max(1, cuts[t - 1] if t else 1), cuts[t]):
                wait_ends(d, step)
            looped(groups * step, groups * (step + 1), functools.partial(z_step, stage), UNROLL_Z)
        passed = until
    for d in range(1, p.inner):
        target = (outer * p.inner + wrap(inner + d, p.inner), col)
        pl.semaphore_signal(met, inc=1, device_id=target, device_id_type=MESH)
    to_scalar.wait()
    looped(0, p.half, functools.partial(y_step, stages[-1]), UNROLL_Y)
    if p.inner > 1:
        pl.semaphore_wait(met, p.inner - 1)

    def target_band(t):
        back = p.bands - 1 - t
        high = (back * (65536 // p.inner + 1)) >> 16
        return wrap(outer + high, p.outer) * p.inner + wrap(inner + back - high * p.inner, p.inner)

    peers = [wrap(col + 1 + c, p.cols) for c in range(p.cols)]

    def number(t, c):
        return peers[c] * p.bands + target_band(t)

    def pick(d, buf):
        at = d * p.halves
        for g in range(p.rows_dest):
            src = pidx[at + g // LANE, g % LANE]
            buf[pl.ds(g * p.pitch, p.tile), :] = planes_ref[pl.ds(src, p.tile), :]

    def turn(d, buf):
        rows = pl.ds(pl.multiple_of(d * p.rows_dest, LANE), p.rows_dest)
        cos = phase_ref[rows, :LANE].astype(f32)
        sin = phase_ref[rows, LANE : 2 * LANE].astype(f32)
        folded = 0.0
        for j in range(p.chunks):
            re = buf[pl.ds(j, p.rows_dest, stride=p.pitch), :]
            im = buf[pl.ds(p.chunks + j, p.rows_dest, stride=p.pitch), :]
            turned = jnp.concatenate([(cos * re - sin * im).astype(bf16), (sin * re + cos * im).astype(bf16)], axis=1)
            part = jnp.dot(turned, fold_ref[...], preferred_element_type=f32)
            folded = folded + (pltpu.roll(part, j * p.chunk_pairs, 1) if j else part)
        folded = folded * phase_ref[rows, 2 * LANE :].astype(f32)
        total = folded[: p.rows_packed]
        for q in range(1, p.pack):
            total = total + pltpu.roll(folded[q * p.rows_packed : (q + 1) * p.rows_packed], q * 2 * p.pairs, 1)
        part_ref[d] = total.astype(bf16)

    def peer(c):
        return (band, peers[c])

    def part_copy(t, c):
        return remote(part_ref.at[number(t, c)], row1.at[c, t], sem1.at[0, c, t], sem1.at[1, c, t], peer(c))

    def block_part_copy(c):
        src = part_ref.at[p.dests, pl.ds(0, p.block_rows)]
        return remote(src, block1.at[c], sem1.at[0, c, p.bands], sem1.at[1, c, p.bands], peer(c))

    def sum_copies(t):
        target = (target_band(t), col)
        return (
            remote(sum_ref.at[t], row_ref.at[band], sem2.at[0, 0, t], sem2.at[1, 0, t], target),
            remote(
                sum_ref.at[p.bands, pl.ds(0, p.block_rows)],
                block_ref.at[band],
                sem2.at[0, 1, t],
                sem2.at[1, 1, t],
                target,
            ),
        )

    def add_up(t):
        total = part_ref[number(t, p.cols - 1)].astype(f32)
        for c in range(p.cols - 1):
            part_copy(t, c).wait_recv()
        for c in range(p.cols - 1):
            total = total + row1[c, t].astype(f32)
        return total.astype(bf16)

    def add_up_block():
        total = part_ref[p.dests, : p.block_rows, :].astype(f32)
        for c in range(p.cols - 1):
            block_part_copy(c).wait_recv()
        for c in range(p.cols - 1):
            total = total + block1[c].astype(f32)
        return total.astype(bf16)

    def when(condition, action):
        pl.when(condition)(action)

    buffers = (pick_a, pick_b)
    pick(p.dests, pick_a)

    def send_sums(t):
        for copy in sum_copies(t):
            copy.start()

    def walk(t, carry):
        for c in range(p.cols):
            pick(number(t, c), buffers[(c + 1) % 2])
            if c == 0:
                turn(jnp.where(t == 0, p.dests, number(t - 1, p.cols - 1)), buffers[0])
                when(t > 0, lambda: part_copy(t - 1, p.cols - 2).start())
            else:
                turn(number(t, c - 1), buffers[c % 2])
                if c > 1:
                    part_copy(t, c - 2).start()
            if c == 1:
                when(t > 2, lambda: send_sums(t - 3))
            if c == min(2, p.cols - 1):

                @pl.when(t == 0)
                def _():
                    for k in range(p.cols - 1):
                        block_part_copy(k).start()

        @pl.when(t == 1)
        def _():
            sum_ref[p.bands, : p.block_rows, :] = add_up_block()

        @pl.when(t > 1)
        def _():
            sum_ref[t - 2] = add_up(t - 2)

        return carry

    lax.fori_loop(0, p.bands, walk, 0)
    last = p.bands - 1
    part_copy(last, p.cols - 2).start()
    sum_ref[last - 1] = add_up(last - 1)
    turn(number(last, p.cols - 1), buffers[0])
    send_sums(last - 2)
    send_sums(last - 1)
    row_ref[band] = add_up(last)
    block_ref[band] = sum_ref[p.bands, : p.block_rows, :]

    pair_lane = lax.broadcasted_iota(i32, (1, LANE), 1)
    pair = lax.rem(pair_lane, p.pairs)
    pair_v, pair_c = lax.rem(pair, p.nv), lax.div(pair, p.nv)

    def spread(which, values):
        out = jnp.zeros((1, LANE), f32)
        for k, value in enumerate(values):
            out = jnp.where(which == k, value, out)
        return out

    valence = [energy_ref[index_ref[i]] for i in range(p.valences)]
    valence = [spread(pair_v, valence[o * p.nv : (o + 1) * p.nv]) for o in range(p.outer)]
    conduction = [
        spread(pair_c, [level_ref[(o * p.inner + i) * p.c_own + l] for o in range(p.outer) for l in range(p.c_own)])
        for i in range(p.inner)
    ]
    norm = 1.0 / math.sqrt(p.valences * p.conductions)
    weights = []
    for b in range(p.bands):
        gap = conduction[b % p.inner] - valence[b // p.inner]
        weights.append([-4.0 * gap / (gap * gap + freq_ref[w] * freq_ref[w]) * norm for w in range(p.freqs)])

    for step in range(p.steps):
        for d in range(p.outer - 1):
            for way in range(2):

                @pl.when(passes(way, d))
                def _():
                    hop(way, d, step).wait_send()

        for d in range(1, p.inner):
            v_copy(d, step).wait_send()

    def close_parts(t, carry):
        for c in range(p.cols - 1):
            part_copy(t, c).wait_send()
        return carry

    lax.fori_loop(0, p.bands, close_parts, 0)
    for c in range(p.cols - 1):
        block_part_copy(c).wait_send()

    def close_sums(t, carry):
        for copy in sum_copies(t):
            copy.wait()
        return carry

    lax.fori_loop(0, p.bands - 1, close_sums, 0)

    group_lanes = 2 * p.pairs
    acc = [jnp.zeros((p.rows_packed, 2 * p.freqs * p.blocks), f32) for _ in range(p.pack)]
    for b in range(p.bands):
        rows = row_ref[b]
        block = block_ref[b].astype(f32)[: p.blocks]
        first = jnp.where(pair_lane < group_lanes, block, 0.0)
        turned = jnp.where(
            pair_lane < p.pairs,
            -pltpu.roll(first, LANE - p.pairs, 1),
            jnp.where(pair_lane < group_lanes, pltpu.roll(first, p.pairs, 1), 0.0),
        )
        parts = []
        for w in range(p.freqs):
            weight = weights[b][w]
            parts += [weight * first, weight * turned]
        right = jnp.concatenate(parts, axis=0)
        for q in range(p.pack):
            shifted = (pltpu.roll(right, q * group_lanes, 1) if q else right).astype(bf16)
            acc[q] = acc[q] + lax.dot_general(
                rows, shifted, (((1,), (1,)), ((), ())), preferred_element_type=f32
            )
    for q in range(p.pack):
        chi_ref[q * p.rows_packed : (q + 1) * p.rows_packed, :] = acc[q]


def run(p, index, energy, conduction, freq, v, c, cells, blocks):
    tables = p.z_tables() + [p.y_table(), p.fold_table()]
    vmem, hbm = pl.BlockSpec(memory_space=pltpu.VMEM), pl.BlockSpec(memory_space=pl.ANY)
    dma = pltpu.SemaphoreType.DMA
    f32, bf16, i32 = jnp.float32, jnp.bfloat16, jnp.int32
    halves_all = (p.dests + 1) * p.halves
    return pl.pallas_call(
        functools.partial(kernel, p),
        out_shape=jax.ShapeDtypeStruct((p.rows_dest, 2 * p.freqs * p.blocks), f32),
        in_specs=[hbm] * (9 + len(tables)),
        out_specs=vmem,
        scratch_shapes=[pltpu.VMEM(t.shape, bf16) for t in tables]
        + [pltpu.SMEM(a.shape, a.dtype) for a in (index, energy, conduction, freq)]
        + [
            pltpu.VMEM((p.chunks, (p.gy + 1) * p.zpitch, LANE), f32),
            pltpu.VMEM(((p.half * p.gy + 1) * p.pitch, LANE), f32),
            pltpu.VMEM(((p.rows_dest + 1) * p.pitch, LANE), f32),
            pltpu.VMEM(((p.rows_dest + 1) * p.pitch, LANE), f32),
            pltpu.VMEM((p.nv, p.slab_x, p.gy * p.gz), bf16),
            pltpu.VMEM((p.nc, p.slab_x, p.gy * p.gz), bf16),
            pltpu.VMEM((p.cols,) + cells.shape, i32),
            pltpu.VMEM((p.cols,) + blocks.shape, i32),
            pltpu.SMEM((p.cols,) + blocks.shape, i32),
            pltpu.VMEM((halves_all, LANE), i32),
            pltpu.SMEM((halves_all, LANE), i32),
            pltpu.VMEM((halves_all, LANE), i32),
            pltpu.VMEM((halves_all * LANE, p.wide), bf16),
            pltpu.VMEM((p.code_rows, p.wide), bf16),
            pltpu.VMEM((p.dests + 1, p.rows_packed, LANE), bf16),
            pltpu.VMEM((p.cols - 1, p.bands, p.rows_packed, LANE), bf16),
            pltpu.VMEM((p.bands + 1, p.rows_packed, LANE), bf16),
            pltpu.VMEM((p.bands, p.rows_packed, LANE), bf16),
            pltpu.VMEM((p.cols - 1, p.block_rows, LANE), bf16),
            pltpu.VMEM((p.bands, p.block_rows, LANE), bf16),
            dma((7,)),
            dma((p.inner - 1, p.steps)),
            dma((p.inner - 1, p.steps)),
            dma((2, p.outer - 1, p.steps)),
            dma((2, p.outer - 1, p.steps)),
            dma((2, 2, p.cols - 1)),
            dma((2, p.cols - 1, p.bands + 1)),
            dma((2, 2, p.bands)),
            pltpu.SemaphoreType.REGULAR,
            dma((len(tables) + 4,)),
        ],
        compiler_params=pltpu.CompilerParams(
            collective_id=0, has_side_effects=True, vmem_limit_bytes=VMEM_LIMIT
        ),
        name="chi",
    )(index, energy, conduction, freq, v, c, cells, blocks, p.x_tables(), *tables)


def per_device(
    valence_wave,
    conduction_wave,
    valence_index,
    occupied_energy,
    conduction_energy,
    frequency,
    gvec_cell,
    block_cell,
):
    cols, bands = lax.axis_size("col"), lax.axis_size("band")
    p = Plan(
        valence_wave.shape[0],
        conduction_wave.shape[0],
        valence_wave.shape[1],
        valence_wave.shape[2],
        cols,
        bands,
        gvec_cell.shape[0] * cols,
        block_cell.shape[0] * cols,
        frequency.shape[0],
    )
    return run(
        p,
        valence_index,
        occupied_energy,
        conduction_energy,
        frequency,
        valence_wave,
        conduction_wave,
        gvec_cell.reshape(-1, LANE),
        block_cell.reshape(1, -1),
    )


def solution(mesh):
    return jax.shard_map(
        per_device,
        mesh=mesh,
        in_specs=(
            P("band", "col", None),
            P("band", "col", None),
            P(),
            P(),
            P(),
            P(),
            P("col"),
            P("col"),
        ),
        out_specs=P(("col", "band"), None),
        check_vma=False,
    )
```
